32 devices in a mesh: dp: 16 (over z, x, core), tensor: 2 (over y).
Axes of the slice: x: 2, y: 2, z: 4, core: 2. Of those that a mesh axis runs over, the one named last changes fastest.
Arguments:
- block_input: bfloat16 [8192, 2048], P('dp'), may hold values from -6 to 6
- segment_ids: int32 [8192], P('dp'), may hold values from 0 to 3, as said below
- position_ids: int32 [8192], P('dp'), may hold values from 0 to 2008, as said below
- attn_gain: bfloat16 [2048], P('dp'), may hold values from 0.099609375 to 1.8984375
- w_query: bfloat16 [2048, 2048], P('dp', 'tensor'), may hold values from -0.09668913 to 0.09668913
- key_projection_weight: bfloat16 [2048, 256], P('dp', 'tensor'), may hold values from -0.09668913 to 0.09668913
- value_projection_weight: bfloat16 [2048, 256], P('dp', 'tensor'), may hold values from -0.125 to 0.125
- w_out: bfloat16 [2048, 2048], P('tensor', 'dp'), may hold values from -1 to 1
- mlp_gain: bfloat16 [2048], P('dp'), may hold values from 0.099609375 to 1.8984375
- w_gate: bfloat16 [2048, 5632], P('dp', 'tensor'), may hold values from -0.125 to 0.125
- w_up: bfloat16 [2048, 5632], P('dp', 'tensor'), may hold values from -0.125 to 0.125
- w_down: bfloat16 [5632, 2048], P('tensor', 'dp'), may hold values from -0.15625 to 0.15625
- out_grad: float32 [8192, 2048], P('dp'), may hold values from -6 to 6
Outputs:
- block_output: float32 [8192, 2048], P('dp')
- input_grad: float32 [8192, 2048], P('dp')
- attn_gain_grad: float32 [2048], P('dp')
- query_weight_grad: float32 [2048, 2048], P('dp', 'tensor')
- key_weight_grad: float32 [2048, 256], P('dp', 'tensor')
- value_weight_grad: float32 [2048, 256], P('dp', 'tensor')
- out_weight_grad: float32 [2048, 2048], P('tensor', 'dp')
- mlp_gain_grad: float32 [2048], P('dp')
- gate_weight_grad: float32 [2048, 5632], P('dp', 'tensor')
- up_weight_grad: float32 [2048, 5632], P('dp', 'tensor')
- down_weight_grad: float32 [5632, 2048], P('tensor', 'dp')
The draws below stay inside these ranges and needn't reach their ends.
Inputs may be any that keep to these rules, and one draw needn't show every extreme that they name: `segment_ids`: each packed sequence of 512 tokens holds four documents in order: numbers 0, 1, 2, 3, each one or more tokens long. `position_ids`: rises by one from token to token within a document and starts at 0 at each document start, except the first document of a sequence, which may continue an earlier one and start higher; the largest position is reached in every draw.
All inputs are finite; a program needn't handle non-finite values.
Results may differ from the reference program's by a relative error of at most 0.015.
The reference program's roundings to bfloat16 on the way count: a program that leaves them out, or rounds other values in their place, can miss the bound.
Values may be sent and summed in bfloat16 or wider, within the bound.
No kernel may reach another device: no remote copies, remote signals or barrier semaphores. Data moves between devices by JAX's collectives and lax.ppermute only.
A program may use at most 320 MiB of HBM per device.

```python
import jax
import jax.numpy as jnp
from jax import lax

MODEL_WIDTH = 2048
QUERY_HEADS = 32
KEY_VALUE_HEADS = 4
HEAD_SIZE = 64
FF = 5632
PACKED_TOKENS = 512
TOKENS = 8192


def document_layout(key):
    rows_count = TOKENS // PACKED_TOKENS
    base_key = jax.random.fold_in(key, 11)
    perm_keys = jax.random.split(jax.random.fold_in(base_key, 1), rows_count)
    orders = jax.vmap(lambda one_key: jax.random.permutation(one_key, PACKED_TOKENS - 1))(perm_keys)
    cuts = jnp.sort(orders[:, :3] + 1, axis=1).astype(jnp.int32)
    index = jnp.arange(PACKED_TOKENS, dtype=jnp.int32)
    segments = jnp.sum((index[None, :, None] >= cuts[:, None, :]).astype(jnp.int32), axis=-1).astype(jnp.int32)
    starts = jnp.concatenate([jnp.zeros((rows_count, 1), jnp.int32), cuts], axis=1)
    first_index = jnp.take_along_axis(starts, segments, axis=1)
    drawn = jax.random.randint(jax.random.fold_in(base_key, 2), (rows_count,), 0, 1501).astype(jnp.int32)
    rows_index = jnp.arange(rows_count, dtype=jnp.int32)
    pinned = (PACKED_TOKENS + 1497 - cuts[:, 0]).astype(jnp.int32)
    offsets = jnp.where(rows_index == 0, pinned, drawn).astype(jnp.int32)
    positions = index[None, :] - first_index + jnp.where(segments == 0, offsets[:, None], 0)
    return (segments.reshape(-1).astype(jnp.int32), positions.reshape(-1).astype(jnp.int32))


def draw_segment_ids(key, part):
    return document_layout(key)[0]


def draw_position_ids(key, part):
    return document_layout(key)[1]


def drawn_weight(key, columns, salt):
    own_key = jax.random.fold_in(key, salt)
    return jax.random.truncated_normal(own_key, -4.0, 4.0, (MODEL_WIDTH, columns), jnp.float32) * MODEL_WIDTH ** (-0.5)


def draw_block_input(key, part):
    noise_key = jax.random.fold_in(key, 31)
    return jax.random.truncated_normal(noise_key, -6.0, 6.0, (TOKENS, MODEL_WIDTH), jnp.float32).astype(jnp.bfloat16)


def draw_w_query(key, part):
    return drawn_weight(key, QUERY_HEADS * HEAD_SIZE, 41).astype(jnp.bfloat16)


def draw_key_projection_weight(key, part):
    return drawn_weight(key, KEY_VALUE_HEADS * HEAD_SIZE, 42).astype(jnp.bfloat16)


def steps_of(stream_key, shape, shards, least, high):
    level, own = 1.0, jax.random.fold_in(stream_key, 6)
    for axis_at, shards_of in shards:
        draws = jnp.exp(jax.random.uniform(jax.random.fold_in(own, axis_at), (shards_of,), jnp.float32, least / len(shards), high / len(shards)))
        level = level * jnp.repeat(draws, shape[axis_at] // shards_of).reshape([-1 if axis == axis_at else 1 for axis in range(len(shape))])
    return level


def scatter_about(rng, extent, scale, bound, shards=(), kind=jnp.bfloat16):
    array = jax.random.normal(rng, extent, jnp.float32) * scale
    if len(shards) > 0:
        array = steps_of(rng, extent, shards, -0.22, 0.18) * array
    return jnp.clip(array, min=-bound, max=bound).astype(kind)


def setup_inputs(seed: int = 0) -> dict:
    streams_of = jax.random.split(jax.random.key(seed), 14)
    return {
        "block_input": draw_block_input(jax.random.fold_in(streams_of[13], 71), 0),
        "segment_ids": draw_segment_ids(jax.random.fold_in(streams_of[13], 71), 0),
        "position_ids": draw_position_ids(jax.random.fold_in(streams_of[13], 71), 0),
        "attn_gain": jnp.clip(1.0 + 0.18 * jax.random.normal(streams_of[3], (MODEL_WIDTH,), jnp.float32), 0.099609375, 1.8984375).astype(jnp.bfloat16),
        "w_query": draw_w_query(jax.random.fold_in(streams_of[13], 71), 0),
        "key_projection_weight": draw_key_projection_weight(jax.random.fold_in(streams_of[13], 71), 0),
        "value_projection_weight": scatter_about(streams_of[6], (MODEL_WIDTH, KEY_VALUE_HEADS * HEAD_SIZE), MODEL_WIDTH ** -0.5, 0.125, ((0, 16), (1, 2))),
        "w_out": scatter_about(streams_of[7], (QUERY_HEADS * HEAD_SIZE, MODEL_WIDTH), (QUERY_HEADS * HEAD_SIZE // 64) ** -0.5, 1.0, ((0, 2), (1, 16))),
        "mlp_gain": jnp.clip(1.0 + 0.18 * jax.random.normal(streams_of[8], (MODEL_WIDTH,), jnp.float32), 0.099609375, 1.8984375).astype(jnp.bfloat16),
        "w_gate": scatter_about(streams_of[9], (MODEL_WIDTH, FF), MODEL_WIDTH ** -0.5, 0.125, ((0, 16), (1, 2))),
        "w_up": scatter_about(streams_of[10], (MODEL_WIDTH, FF), MODEL_WIDTH ** -0.5, 0.125, ((0, 16), (1, 2))),
        "w_down": scatter_about(streams_of[11], (FF, MODEL_WIDTH), (FF // 4) ** -0.5, 0.15625, ((0, 2), (1, 16))),
        "out_grad": scatter_about(streams_of[12], (TOKENS, MODEL_WIDTH), 1.0, 6.0, ((0, 16),), jnp.float32),
    }


EPSILON = 1e-05
MASKED = -1e+30

def normalize(values):
    inverse = lax.rsqrt(lax.optimization_barrier(jnp.mean(values * values, axis=-1, keepdims=True)) + EPSILON)
    return (values * inverse, inverse)

def rotary_tables(positions):
    half_dim = HEAD_SIZE // 2
    frequency = 10000.0 ** (-(jnp.arange(half_dim, dtype=jnp.float32) * 2.0 / HEAD_SIZE))
    angles = positions.astype(jnp.float32)[:, None] * frequency[None, :]
    cosine_table = jnp.cos(angles)
    sine_table = jnp.sin(angles)
    return (jnp.concatenate([cosine_table, cosine_table], -1)[:, None, :], jnp.concatenate([sine_table, sine_table], -1)[:, None, :])

def rotate_halves(values):
    half_dim = values.shape[-1] // 2
    return jnp.concatenate([-values[..., half_dim:], values[..., :half_dim]], -1)

def reference(block_input, segment_ids, position_ids, attn_gain, w_query, key_projection_weight, value_projection_weight, w_out, mlp_gain, w_gate, w_up, w_down, out_grad):
    rows_count = TOKENS // PACKED_TOKENS
    query_group_size = QUERY_HEADS // KEY_VALUE_HEADS
    scaling = HEAD_SIZE ** (-0.5)

    def one_sequence(totals, batch):
        tokens_in, segments, positions, grad_out = batch
        residual_in = tokens_in.astype(jnp.float32)
        normed_one, inverse_one = normalize(residual_in)
        first_hidden_state = (normed_one * attn_gain.astype(jnp.float32)).astype(jnp.bfloat16)
        cosine_table, sine_table = rotary_tables(positions)
        query_raw = jnp.dot(first_hidden_state, w_query, preferred_element_type=jnp.float32).reshape(PACKED_TOKENS, QUERY_HEADS, HEAD_SIZE)
        query_rows = (query_raw * cosine_table + rotate_halves(query_raw) * sine_table).astype(jnp.bfloat16)
        key_unrotated = jnp.dot(first_hidden_state, key_projection_weight, preferred_element_type=jnp.float32).reshape(PACKED_TOKENS, KEY_VALUE_HEADS, HEAD_SIZE)
        keys_rot = (key_unrotated * cosine_table + rotate_halves(key_unrotated) * sine_table).astype(jnp.bfloat16)
        value_input_rows = jnp.dot(first_hidden_state, value_projection_weight, preferred_element_type=jnp.float32).astype(jnp.bfloat16).reshape(PACKED_TOKENS, KEY_VALUE_HEADS, HEAD_SIZE)
        grouped_query_rows = query_rows.reshape(PACKED_TOKENS, KEY_VALUE_HEADS, query_group_size, HEAD_SIZE).astype(jnp.float32)
        key_float = keys_rot.astype(jnp.float32)
        value_float = value_input_rows.astype(jnp.float32)
        index = jnp.arange(PACKED_TOKENS)
        allowed = (segments[:, None] == segments[None, :]) & (index[None, :] <= index[:, None])
        scores = jnp.einsum('ikgd,jkd->kgij', grouped_query_rows, key_float) * scaling
        scores = jnp.where(allowed, scores, MASKED)
        peak = lax.optimization_barrier(jnp.max(scores, axis=-1, keepdims=True))
        log_total = peak + jnp.log(lax.optimization_barrier(jnp.sum(jnp.exp(scores - peak), axis=-1, keepdims=True)))
        weights_soft = jnp.exp(scores - log_total)
        probability = lax.optimization_barrier(weights_soft.astype(jnp.bfloat16)).astype(jnp.float32)
        attention_result = jnp.einsum('kgij,jkd->ikgd', probability, value_float).reshape(PACKED_TOKENS, QUERY_HEADS * HEAD_SIZE).astype(jnp.bfloat16)
        middle = residual_in + jnp.dot(attention_result, w_out, preferred_element_type=jnp.float32)
        normed_two, inverse_two = normalize(middle)
        hidden_two = (normed_two * mlp_gain.astype(jnp.float32)).astype(jnp.bfloat16)
        gate_pre = jnp.dot(hidden_two, w_gate, preferred_element_type=jnp.float32)
        up_pre = jnp.dot(hidden_two, w_up, preferred_element_type=jnp.float32)
        sigma = jax.nn.sigmoid(gate_pre)
        swish = gate_pre * sigma
        activation = (swish * up_pre).astype(jnp.bfloat16)
        output = middle + jnp.dot(activation, w_down, preferred_element_type=jnp.float32)
        grad_low = grad_out.astype(jnp.bfloat16)
        down_wgrad = jnp.dot(activation.T, grad_low, preferred_element_type=jnp.float32)
        act_grad = jnp.dot(grad_low, w_down.T, preferred_element_type=jnp.float32)
        gate_back = (act_grad * up_pre * sigma * (1.0 + gate_pre * (1.0 - sigma))).astype(jnp.bfloat16)
        up_back = (act_grad * swish).astype(jnp.bfloat16)
        gate_wgrad = jnp.dot(hidden_two.T, gate_back, preferred_element_type=jnp.float32)
        up_wgrad = jnp.dot(hidden_two.T, up_back, preferred_element_type=jnp.float32)
        hidden_two_grad = jnp.dot(gate_back, w_gate.T, preferred_element_type=jnp.float32) + jnp.dot(up_back, w_up.T, preferred_element_type=jnp.float32)
        mlp_gain_grad = lax.optimization_barrier(jnp.sum(hidden_two_grad * normed_two, axis=0))
        normed_grad = hidden_two_grad * mlp_gain.astype(jnp.float32)
        middle_grad = grad_out + inverse_two * (normed_grad - normed_two * lax.optimization_barrier(jnp.mean(normed_grad * normed_two, axis=-1, keepdims=True)))
        middle_low = middle_grad.astype(jnp.bfloat16)
        out_wgrad = jnp.dot(attention_result.T, middle_low, preferred_element_type=jnp.float32)
        attention_result_narrow = jnp.dot(middle_low, w_out.T, preferred_element_type=jnp.float32).astype(jnp.bfloat16)
        attention_result_gradient = lax.optimization_barrier(attention_result_narrow).reshape(PACKED_TOKENS, KEY_VALUE_HEADS, query_group_size, HEAD_SIZE).astype(jnp.float32)
        row_correction_terms = lax.optimization_barrier(jnp.sum(attention_result_gradient * attention_result.reshape(PACKED_TOKENS, KEY_VALUE_HEADS, query_group_size, HEAD_SIZE).astype(jnp.float32), axis=-1))
        row_correction_terms = jnp.transpose(row_correction_terms, (1, 2, 0))[..., None]
        prob_grad = jnp.einsum('ikgd,jkd->kgij', attention_result_gradient, value_float)
        score_back = lax.optimization_barrier((weights_soft * (prob_grad - row_correction_terms)).astype(jnp.bfloat16)).astype(jnp.float32)
        value_gradient = jnp.einsum('kgij,ikgd->jkd', probability, attention_result_gradient)
        query_grad = jnp.einsum('kgij,jkd->ikgd', score_back, key_float).reshape(PACKED_TOKENS, QUERY_HEADS, HEAD_SIZE) * scaling
        key_gradient = jnp.einsum('kgij,ikgd->jkd', score_back, grouped_query_rows) * scaling
        query_back = (query_grad * cosine_table - rotate_halves(query_grad) * sine_table).astype(jnp.bfloat16).reshape(PACKED_TOKENS, QUERY_HEADS * HEAD_SIZE)
        key_backward_rows = (key_gradient * cosine_table - rotate_halves(key_gradient) * sine_table).astype(jnp.bfloat16).reshape(PACKED_TOKENS, KEY_VALUE_HEADS * HEAD_SIZE)
        value_backward_rows = value_gradient.astype(jnp.bfloat16).reshape(PACKED_TOKENS, KEY_VALUE_HEADS * HEAD_SIZE)
        query_wgrad = jnp.dot(first_hidden_state.T, query_back, preferred_element_type=jnp.float32)
        key_wgrad = jnp.dot(first_hidden_state.T, key_backward_rows, preferred_element_type=jnp.float32)
        value_wgrad = jnp.dot(first_hidden_state.T, value_backward_rows, preferred_element_type=jnp.float32)
        hidden_one_grad = jnp.dot(query_back, w_query.T, preferred_element_type=jnp.float32)
        hidden_one_grad = hidden_one_grad + jnp.dot(key_backward_rows, key_projection_weight.T, preferred_element_type=jnp.float32)
        hidden_one_grad = hidden_one_grad + jnp.dot(value_backward_rows, value_projection_weight.T, preferred_element_type=jnp.float32)
        attn_gain_grad = lax.optimization_barrier(jnp.sum(hidden_one_grad * normed_one, axis=0))
        normed_one_grad = hidden_one_grad * attn_gain.astype(jnp.float32)
        input_grad = middle_grad + inverse_one * (normed_one_grad - normed_one * lax.optimization_barrier(jnp.mean(normed_one_grad * normed_one, axis=-1, keepdims=True)))
        terms = (attn_gain_grad, query_wgrad, key_wgrad, value_wgrad, out_wgrad, mlp_gain_grad, gate_wgrad, up_wgrad, down_wgrad)
        new_totals = tuple((total + term for total, term in zip(totals, terms)))
        return (new_totals, (output, input_grad))
    shapes = (attn_gain, w_query, key_projection_weight, value_projection_weight, w_out, mlp_gain, w_gate, w_up, w_down)
    starting = tuple((jnp.zeros(weight.shape, jnp.float32) for weight in shapes))
    batches = (block_input.reshape(rows_count, PACKED_TOKENS, MODEL_WIDTH), segment_ids.reshape(rows_count, PACKED_TOKENS), position_ids.reshape(rows_count, PACKED_TOKENS), out_grad.reshape(rows_count, PACKED_TOKENS, MODEL_WIDTH))
    totals, (outputs, input_grads) = lax.scan(one_sequence, starting, batches)
    return (outputs.reshape(TOKENS, MODEL_WIDTH), input_grads.reshape(TOKENS, MODEL_WIDTH), totals[0], totals[1], totals[2], totals[3], totals[4], totals[5], totals[6], totals[7], totals[8])
```

```python
import functools
import math

import jax
import jax.numpy as jnp
from jax import lax
from jax.experimental import pallas as pl
from jax.experimental.pallas import tpu as pltpu
from jax.sharding import PartitionSpec as P


fixed = lax.optimization_barrier

HEAD_SIZE = 64
EPSILON = 1e-05
MASKED = -1e30
LANES = 128
F32 = jnp.float32
BF16 = jnp.bfloat16


def dot(a, b, ca, cb, out=F32):
    return lax.dot_general(a, b, (((ca,), (cb,)), ((), ())), preferred_element_type=out)


def cost(flops, moved, exps=0):
    return pl.CostEstimate(flops=int(flops), bytes_accessed=int(moved), transcendentals=int(exps))


def params(count=1):
    return pltpu.CompilerParams(
        dimension_semantics=("arbitrary",) * count, vmem_limit_bytes=60 * 1024 * 1024
    )


def normalize(values):
    inverse = lax.rsqrt(jnp.mean(values * values, axis=-1, keepdims=True) + EPSILON)
    return (values * inverse, inverse)


def tile_of(width, most):
    tile = most
    while width % tile:
        tile //= 2
    return tile


class Ring:
    def __init__(self, dp, tensor):
        self.dp, self.tensor, self.width = dp, tensor, None
        self.cores = self.pairs = 2
        self.groups = dp // 4

    def at(self, g, p, c):
        return (g * self.pairs + p) * self.cores + c

    def members(self):
        return [
            (g, p, c)
            for g in range(self.groups)
            for p in range(self.pairs)
            for c in range(self.cores)
        ]

    def move(self, value, where):
        return lax.ppermute(
            value, "dp", [(self.at(*m), self.at(*where(*m))) for m in self.members()]
        )

    def swap_core(self, value):
        return self.move(value, lambda g, p, c: (g, p, 1 - c))

    def swap_pair(self, value):
        return self.move(value, lambda g, p, c: (g, 1 - p, c))

    def shift_group(self, value, shift):
        return self.move(value, lambda g, p, c: ((g + shift) % self.groups, p, c))

    def column_list(self):
        return [
            [self.at(g, p, c) for g in range(self.groups) for c in range(self.cores)]
            for p in range(self.pairs)
        ]

    def group_list(self):
        return [
            [self.at(g, p, c) for g in range(self.groups)]
            for p in range(self.pairs)
            for c in range(self.cores)
        ]


def rotate(values, cosine, signed_sine, lane):
    ahead = pltpu.roll(values, LANES - HEAD_SIZE // 2, 1)
    behind = pltpu.roll(values, HEAD_SIZE // 2, 1)
    crossed = jnp.where(lane % HEAD_SIZE < HEAD_SIZE // 2, ahead, behind)
    return values * cosine + crossed * signed_sine


def twice(values, second, lane):
    other = pltpu.roll(values, HEAD_SIZE, 1)
    low = lane < HEAD_SIZE
    return jnp.where(second, jnp.where(low, other, values), jnp.where(low, values, other))


def attention_forward_kernel(
    per_kv, tile, q_ref, k_ref, v_ref, cos_ref, sin_ref, seg_row, seg_col,
    q_out, k_out, v_out, o_ref, lse_ref, mask,
):
    step = pl.program_id(0)
    tokens = q_ref.shape[0]
    lane = lax.broadcasted_iota(jnp.int32, (tokens, LANES), 1)
    scale = HEAD_SIZE**-0.5

    @pl.when(step == 0)
    def _():
        row = lax.broadcasted_iota(jnp.int32, (tokens, tokens), 0)
        col = lax.broadcasted_iota(jnp.int32, (tokens, tokens), 1)
        allowed = (seg_col[...] == seg_row[...]) & (col <= row)
        mask[...] = jnp.where(allowed, 0.0, MASKED)
        k_out[...] = rotate(k_ref[...], cos_ref[...], sin_ref[...], lane).astype(BF16)
        v_out[...] = v_ref[...].astype(BF16)
        lse_ref[...] = jnp.zeros_like(lse_ref)

    second = step // per_kv == 1
    low = lane < HEAD_SIZE
    query = rotate(q_ref[...], cos_ref[...], sin_ref[...], lane)
    q_out[...] = query.astype(BF16)
    keys = twice(k_out[...].astype(F32), second, lane).astype(BF16)
    value = twice(v_out[...].astype(F32), second, lane)
    for start in range(0, tokens, tile):
        seen = start + tile
        total = jnp.zeros((tile, LANES), F32)
        for half in range(2):
            inside = low if half == 0 else ~low
            part = jnp.where(inside[:tile], query[start:seen], 0.0).astype(BF16)
            scores = dot(part, keys[:seen], 1, 1) * scale + mask[start:seen, :seen]
            peak = jnp.max(scores, axis=1, keepdims=True)
            weights = jnp.exp(scores - peak)
            norm = jnp.sum(weights, axis=1, keepdims=True)
            probability = (weights / norm).astype(BF16)
            shown = jnp.where(inside, value, 0.0).astype(BF16)
            total += dot(probability, shown[:seen], 1, 0)
            log_total = peak + jnp.log(norm)
            here = lane[:tile] == 2 * step + half
            lse_ref[start:seen, :] = jnp.where(here, log_total, lse_ref[start:seen, :])
        o_ref[start:seen, :] = total.astype(BF16)


def attention_forward(qkv, cosine, signed_sine, segments, heads, kv_heads):
    tokens = qkv.shape[0]
    steps = heads // 2
    tile = tile_of(tokens, 256)
    fixed = lambda j: (0, 0)
    block = (tokens, LANES)
    scores = heads * tokens * tokens
    return pl.pallas_call(
        functools.partial(attention_forward_kernel, steps // kv_heads, tile),
        grid=(steps,),
        in_specs=[
            pl.BlockSpec(block, lambda j: (0, j)),
            pl.BlockSpec(block, lambda j: (0, steps)),
            pl.BlockSpec(block, lambda j: (0, steps + 1)),
            pl.BlockSpec(block, fixed),
            pl.BlockSpec(block, fixed),
            pl.BlockSpec((1, tokens), fixed),
            pl.BlockSpec((tokens, 1), fixed),
        ],
        out_specs=[
            pl.BlockSpec(block, lambda j: (0, j)),
            pl.BlockSpec(block, fixed),
            pl.BlockSpec(block, fixed),
            pl.BlockSpec(block, lambda j: (0, j)),
            pl.BlockSpec(block, fixed),
        ],
        out_shape=[
            jax.ShapeDtypeStruct((tokens, heads * HEAD_SIZE), BF16),
            jax.ShapeDtypeStruct(block, BF16),
            jax.ShapeDtypeStruct(block, BF16),
            jax.ShapeDtypeStruct((tokens, heads * HEAD_SIZE), BF16),
            jax.ShapeDtypeStruct(block, F32),
        ],
        scratch_shapes=[pltpu.VMEM((tokens, tokens), F32)],
        compiler_params=params(),
        cost_estimate=cost(4 * scores * HEAD_SIZE, 6 * tokens * qkv.shape[1], scores),
        name="attention_forward",
    )(qkv, qkv, qkv, cosine, signed_sine, segments[None, :], segments[:, None])


def attention_backward_kernel(
    steps, per_kv, tile, q_ref, k_ref, v_ref, o_ref, do_ref, lse_ref, cos_ref, sin_ref,
    seg_row, seg_col, out_ref, mask, key_part, value_part, key_all, value_all,
):
    step = pl.program_id(0)
    tokens = q_ref.shape[0]
    lane = lax.broadcasted_iota(jnp.int32, (tokens, LANES), 1)
    low = lane < HEAD_SIZE
    scale = HEAD_SIZE**-0.5

    @pl.when(step == 0)
    def _():
        row = lax.broadcasted_iota(jnp.int32, (tokens, tokens), 0)
        col = lax.broadcasted_iota(jnp.int32, (tokens, tokens), 1)
        allowed = (seg_col[...] == seg_row[...]) & (col <= row)
        mask[...] = jnp.where(allowed, 0.0, MASKED)

    @pl.when((step % per_kv == 0) & (step < steps))
    def _():
        key_part[...] = jnp.zeros_like(key_part)
        value_part[...] = jnp.zeros_like(value_part)

    @pl.when(step < steps)
    def _():
        second = step // per_kv == 1
        keys = twice(k_ref[...].astype(F32), second, lane)
        value = twice(v_ref[...].astype(F32), second, lane).astype(BF16)
        keys_low = keys.astype(BF16)
        given = do_ref[...].astype(F32)
        product = given * o_ref[...].astype(F32)
        query = q_ref[...].astype(F32)
        for start in range(0, tokens, tile):
            seen = start + tile
            total = jnp.zeros((tile, LANES), F32)
            for half in range(2):
                inside = low if half == 0 else ~low
                near = inside[:tile]
                part = jnp.where(near, query[start:seen], 0.0).astype(BF16)
                grad = jnp.where(near, given[start:seen], 0.0).astype(BF16)
                terms = jnp.sum(
                    jnp.where(near, product[start:seen], 0.0), axis=1, keepdims=True
                )
                here = lane[:tile] == 2 * step + half
                log_total = jnp.sum(
                    jnp.where(here, lse_ref[start:seen, :], 0.0), axis=1, keepdims=True
                )
                scores = dot(part, keys_low[:seen], 1, 1) * scale + mask[start:seen, :seen]
                weights = jnp.exp(scores - log_total)
                slope = dot(grad, value[:seen], 1, 1)
                back = (weights * (slope - terms)).astype(BF16)
                shown = jnp.where(inside, keys, 0.0).astype(BF16)
                total += dot(back, shown[:seen], 1, 0)
                key_part[:seen, :] += dot(back, part, 0, 0)
                value_part[:seen, :] += dot(weights.astype(BF16), grad, 0, 0)
            out_ref[start:seen, :] = rotate(
                total * scale, cos_ref[start:seen, :], -sin_ref[start:seen, :], lane[:tile]
            ).astype(BF16)

    @pl.when((step % per_kv == per_kv - 1) & (step < steps))
    def _():
        here = low == (step // per_kv == 0)
        for part, total in ((key_part, key_all), (value_part, value_all)):
            folded = part[...] + pltpu.roll(part[...], HEAD_SIZE, 1)
            total[...] = jnp.where(here, folded, total[...])

    @pl.when(step == steps)
    def _():
        out_ref[...] = rotate(
            key_all[...] * scale, cos_ref[...], -sin_ref[...], lane
        ).astype(BF16)

    @pl.when(step == steps + 1)
    def _():
        out_ref[...] = value_all[...].astype(BF16)


def attention_backward(
    query, keys, value, attended, attended_grad, log_total, cosine, signed_sine, segments, kv_heads
):
    tokens, width = query.shape
    steps = width // LANES
    tile = tile_of(tokens, 256)
    fixed = lambda j: (0, 0)
    moving = lambda j: (0, jnp.minimum(j, steps - 1))
    block = (tokens, LANES)
    scores = width // HEAD_SIZE * tokens * tokens
    return pl.pallas_call(
        functools.partial(attention_backward_kernel, steps, steps // kv_heads, tile),
        grid=(steps + 2,),
        in_specs=[
            pl.BlockSpec(block, moving),
            pl.BlockSpec(block, fixed),
            pl.BlockSpec(block, fixed),
            pl.BlockSpec(block, moving),
            pl.BlockSpec(block, moving),
            pl.BlockSpec(block, fixed),
            pl.BlockSpec(block, fixed),
            pl.BlockSpec(block, fixed),
            pl.BlockSpec((1, tokens), fixed),
            pl.BlockSpec((tokens, 1), fixed),
        ],
        out_specs=pl.BlockSpec(block, lambda j: (0, j)),
        out_shape=jax.ShapeDtypeStruct((tokens, width + 2 * LANES), BF16),
        scratch_shapes=[pltpu.VMEM((tokens, tokens), F32)] + [pltpu.VMEM(block, F32)] * 4,
        compiler_params=params(),
        cost_estimate=cost(10 * scores * HEAD_SIZE, 8 * tokens * width, scores),
        name="attention_backward",
    )(
        query, keys, value, attended, attended_grad, log_total, cosine, signed_sine,
        segments[None, :], segments[:, None],
    )


def gathered_order(ring, width):
    rows = ring.width // ring.dp
    block = ring.pairs * ring.cores
    places = []
    for begin in range(0, width // rows, block):
        for p in range(ring.pairs):
            for c in range(ring.cores):
                places.append((begin + p * ring.cores + c, begin + c * ring.pairs + p))
    return [(slice(a * rows, (a + 1) * rows), slice(b * rows, (b + 1) * rows)) for a, b in places]


def hidden_kernel(ring, pieces, *refs):
    gate_ref, up_ref, down_ref, out, hidden, given = refs[pieces:]

    @pl.when(pl.program_id(0) == 0)
    def _():
        for held, parts in ((hidden, refs[: pieces - 2]), (given, refs[pieces - 2 : pieces])):
            at = 0
            for part in parts:
                for place, found in gathered_order(ring, part.shape[1]):
                    held[at : at + part.shape[0], found] = part[:, place]
                at += part.shape[0]

    for begin in range(0, out.shape[2], 256):
        here = slice(begin, min(begin + 256, out.shape[2]))
        gate = dot(hidden[...], gate_ref[:, here], 1, 0)
        up = dot(hidden[...], up_ref[:, here], 1, 0)
        grad = dot(given[...], down_ref[:, here], 1, 0)
        sigma = jax.nn.sigmoid(gate)
        swish = gate * sigma
        out[0, :, here] = (swish * up).astype(BF16)
        out[1, :, here] = (grad * up * sigma * (1.0 + gate * (1.0 - sigma))).astype(BF16)
        out[2, :, here] = (grad * swish).astype(BF16)


def hidden_units(ring, hidden_two, grad_low, weights):
    tokens, width = sum(part.shape[0] for part in grad_low), weights.shape[0]
    units = weights.shape[-1] // 3
    tile = 256 if units % 256 == 0 else units
    count = units // tile
    pieces = [*hidden_two, *grad_low]

    def columns(part):
        buffers = pl.Buffered(1 if count == 1 else 2)
        return pl.BlockSpec(
            (width, tile), lambda j: (0, part * count + j), pipeline_mode=buffers
        )

    return pl.pallas_call(
        functools.partial(hidden_kernel, ring, len(pieces)),
        grid=(count,),
        in_specs=[
            pl.BlockSpec(part.shape, lambda j: (0, 0), pipeline_mode=pl.Buffered(1))
            for part in pieces
        ]
        + [columns(0), columns(1), columns(2)],
        out_specs=pl.BlockSpec((3, tokens, tile), lambda j: (0, 0, j)),
        out_shape=jax.ShapeDtypeStruct((3, tokens, units), BF16),
        scratch_shapes=[pltpu.VMEM((tokens, width), BF16)] * 2,
        compiler_params=params(),
        cost_estimate=cost(6 * tokens * width * units, 6 * width * units, tokens * units),
        name="hidden_units",
    )(*pieces, weights, weights, weights)


def back_kernel(ring, parts, has_start, *refs):
    values, weights = refs[:parts], refs[parts : 2 * parts]
    total = dot(values[0][...], weights[0][...], 1, 1)
    for value, weight in zip(values[1:], weights[1:]):
        total += dot(value[...], weight[...], 1, 1)
    tokens = refs[-1].shape[0]
    for at, out in ((0, refs[-2]), (1, refs[-1])):
        for place, found in gathered_order(ring, out.shape[1]):
            part = total[at * tokens : (at + 1) * tokens, found]
            if has_start:
                part += refs[2 * parts + at][:, place]
            out[:, place] = part.astype(out.dtype)


def back_project(ring, values, picks, weights, first, start, dtype, piece=0, pieces=1):
    _, both, units = values.shape
    tokens = both // 2
    width = weights.shape[0]
    tile = min(512, width // pieces)
    count = width // pieces // tile
    parts = len(picks)

    def chosen(pick):
        return pl.BlockSpec((None, both, units), lambda j: (pick, 0, 0))

    def columns(part):
        return pl.BlockSpec((tile, units), lambda j: (piece * count + j, first + part))

    begin = pl.BlockSpec((tokens, tile), lambda j: (0, piece * count + j))
    return pl.pallas_call(
        functools.partial(back_kernel, ring, parts, start is not None),
        grid=(count,),
        in_specs=[chosen(pick) for pick in picks]
        + [columns(i) for i in range(parts)]
        + ([begin] * 2 if start is not None else []),
        out_specs=[pl.BlockSpec((tokens, tile), lambda j: (0, j))] * 2,
        out_shape=[jax.ShapeDtypeStruct((tokens, count * tile), dtype)] * 2,
        compiler_params=params(),
        cost_estimate=cost(
            2 * both * width * units * parts // pieces, 2 * width * units * parts // pieces
        ),
        name="back_project",
    )(*([values] * parts), *([weights] * parts), *(start if start is not None else ()))


def transpose_kernel(*refs):
    refs[-1][...] = jnp.concatenate([ref[...] for ref in refs[:-1]], 0).T


def transposed(values):
    tokens, width = values[0].shape
    tile = tile_of(width, 512)
    count = len(values)
    return pl.pallas_call(
        transpose_kernel,
        grid=(width // tile,),
        in_specs=[pl.BlockSpec((tokens, tile), lambda j: (0, j))] * count,
        out_specs=pl.BlockSpec((tile, count * tokens), lambda j: (j, 0)),
        out_shape=jax.ShapeDtypeStruct((width, count * tokens), values[0].dtype),
        compiler_params=params(),
        cost_estimate=cost(0, 4 * tokens * width * count),
        name="transposed",
    )(*values)


def grad_kernel(layout, lefts, rights, has_extra, pieces, where, *refs):
    own_left, got_left = refs[:lefts], refs[lefts : 2 * lefts]
    own_right = refs[2 * lefts : 2 * lefts + rights]
    got_right = refs[2 * lefts + rights : 2 * lefts + 2 * rights]
    step = pl.program_id(0)
    rows, tokens = own_left[0].shape[-2:]
    height = own_left[0].shape[0] * own_left[0].shape[1] * rows
    for left, right, begin, end in layout:

        @pl.when((step >= begin) & (step < end))
        def _():
            shape = (height, tokens)
            total = dot(own_left[left][...].reshape(shape), own_right[right][...], 1, 0)
            total += dot(got_left[left][...].reshape(shape), got_right[right][...], 1, 0)
            if has_extra:
                total += refs[2 * lefts + 2 * rights][...].astype(F32)
            if pieces == 0:
                refs[-1][...] = total.astype(BF16)
                return
            outs, held = refs[-pieces - 1 : -1], refs[-1]
            held[...] = total
            for shift, out in enumerate(outs):
                start = pl.multiple_of(where[2 + shift] * rows, rows)
                out[...] = held[pl.ds(start, rows), :].astype(BF16)


def weight_grad(where, own_left, got_left, rights, extra=None, split=False, whole=False):
    groups, pairs, _, rows, tokens = own_left[0].shape
    taken = pairs if whole else 1
    height = groups * taken * rows
    tile = math.gcd(*(own.shape[-1] for _, own, _, _ in rights))
    tile //= next(n for n in range(1, tile) if tile // n <= (768 if whole else 1536) and tile % (n * LANES) == 0)
    layout, columns, begin = [], [], 0
    for k, (left, own, _, pick) in enumerate(rights):
        count = own.shape[-1] // tile
        layout.append((left, k, begin, begin + count))
        columns.append(
            pl.BlockSpec(
                (None, tokens, tile),
                functools.partial(
                    lambda j, w, p, b, n: (p, 0, jnp.clip(j - b, 0, n - 1)),
                    p=pick,
                    b=begin,
                    n=count,
                ),
            )
        )
        begin += count
    own = pl.BlockSpec(
        (groups, taken, 1, rows, tokens), lambda j, w: (0, 0 if whole else w[0], w[1], 0, 0)
    )
    got = pl.BlockSpec(
        (groups, taken, rows, tokens), lambda j, w: (0, 0 if whole else w[0], 0, 0)
    )
    out = pl.BlockSpec((height, tile), lambda j, w: (0, j))
    args = [*own_left, *got_left, *(r[1] for r in rights), *(r[2] for r in rights)]
    specs = [own] * len(own_left) + [got] * len(got_left) + columns * 2
    shapes = jax.ShapeDtypeStruct((height, begin * tile), BF16)
    outs, scratch, pieces = out, [], 0
    if extra is not None:
        args.append(extra)
        specs.append(out)
    if split:
        pieces = groups
        outs = [pl.BlockSpec((rows, tile), lambda j, w: (0, j))] * groups
        shapes = [jax.ShapeDtypeStruct((rows, begin * tile), BF16)] * groups
        scratch = [pltpu.VMEM((height, tile), F32)]
    return pl.pallas_call(
        functools.partial(
            grad_kernel, tuple(layout), len(own_left), len(rights), extra is not None, pieces
        ),
        grid_spec=pltpu.PrefetchScalarGridSpec(
            num_scalar_prefetch=1,
            grid=(begin,),
            in_specs=specs,
            out_specs=outs,
            scratch_shapes=scratch,
        ),
        out_shape=shapes,
        compiler_params=params(),
        cost_estimate=cost(
            4 * height * tokens * begin * tile, 2 * (height + 2 * tokens) * begin * tile
        ),
        name="weight_grad",
    )(where, *args)


def per_device(
    ring,
    block_input,
    segment_ids,
    position_ids,
    attn_gain,
    w_query,
    key_projection_weight,
    value_projection_weight,
    w_out,
    mlp_gain,
    w_gate,
    w_up,
    w_down,
    out_grad,
):
    seq_len, width = block_input.shape
    ring.width = width
    rows = w_query.shape[0]
    q_cols, kv_cols = w_query.shape[1], key_projection_weight.shape[1]
    heads, kv_heads = q_cols // HEAD_SIZE, kv_cols // HEAD_SIZE
    hidden = w_gate.shape[1]
    me = lax.axis_index("dp")
    core = me % ring.cores
    pair = (me // ring.cores) % ring.pairs
    my_group = me // (ring.cores * ring.pairs)

    def tensor_sum(low, after=None):
        if ring.tensor == 2:
            other = lax.ppermute(low, "tensor", [(0, 1), (1, 0)])
            if after is not None:
                other = fixed((other, after))[0]
            return low.astype(F32) + other.astype(F32)
        return lax.psum(low, "tensor").astype(F32)

    gains = jnp.pad(jnp.stack([attn_gain, mlp_gain], 1), ((0, 0), (0, LANES - 2)))
    qkv_cols = q_cols + 2 * kv_cols
    first = lax.all_gather(
        jnp.concatenate(
            [w_query, key_projection_weight, value_projection_weight, w_out.T, gains], 1
        ),
        "dp",
        axis=0,
        tiled=True,
    )
    half = hidden // ring.pairs
    cut = (half // LANES * 6 // 11) * LANES
    bounds = ((0, cut), (cut, half))
    local = jnp.stack([w_gate, w_up, w_down.T], 1).reshape(rows, 3, ring.pairs, half)

    def of_pair(index):
        return lax.dynamic_index_in_dim(local, index, 2, keepdims=False)

    kept = of_pair(pair)
    sent = ring.swap_pair(of_pair(1 - pair))
    both = jnp.stack([jnp.where(pair == 0, kept, sent), jnp.where(pair == 0, sent, kept)], 0)
    weights_a, weights_b = [
        lax.all_gather(
            both[..., a:b].reshape(ring.pairs * rows, 3 * (b - a)),
            "dp",
            axis=0,
            tiled=True,
            axis_index_groups=ring.column_list(),
        )
        for a, b in bounds
    ]
    full_qkv = first[:, :qkv_cols]
    out_t = first[:, qkv_cols : qkv_cols + w_out.shape[0]]
    gain_rows = first[:, qkv_cols + w_out.shape[0] :].T.astype(F32)
    gain_one, gain_two = gain_rows[0], gain_rows[1]

    def left_side(*values):
        own = transposed(values).reshape(ring.groups, ring.pairs, ring.cores, rows, -1)
        give = lax.dynamic_index_in_dim(own, 1 - core, 2, keepdims=False)
        return own, ring.swap_core(give)

    targets = [(my_group + shift) % ring.groups for shift in range(ring.groups)]
    far = jnp.stack([1 - pair, core, *targets]).astype(jnp.int32)
    near = jnp.stack([pair, core, *targets]).astype(jnp.int32)

    residual_in = block_input.astype(F32)
    normed_one, inverse_one = normalize(residual_in)
    hidden_one = fixed((normed_one * gain_one).astype(BF16))
    half_dim = HEAD_SIZE // 2
    frequency = 10000.0 ** (-(jnp.arange(half_dim, dtype=F32) * 2.0 / HEAD_SIZE))
    angles = position_ids.astype(F32)[:, None] * frequency[None, :]
    cosine, sine = jnp.cos(angles), jnp.sin(angles)
    cosine = jnp.concatenate([cosine] * 4, 1)
    signed_sine = jnp.concatenate([-sine, sine, -sine, sine], 1)
    qkv = dot(hidden_one, full_qkv, 1, 0)

    def both_pairs(values):
        return values, ring.swap_pair(values)

    grad_low = both_pairs(fixed((out_grad.astype(BF16), qkv))[0])
    grad_left = left_side(*grad_low)
    query, keys, value, attended, log_total = attention_forward(
        qkv, cosine, signed_sine, segment_ids, heads, kv_heads
    )
    attended_got = ring.swap_core(attended)
    one_left = left_side(hidden_one)
    middles, hiddens = [], []
    for k in range(2):
        part = slice(k * seq_len // 2, (k + 1) * seq_len // 2)
        low = dot(attended[part], out_t, 1, 1, BF16)
        middles.append(residual_in[part] + tensor_sum(low, hiddens[-1][0] if k else None))
        hidden_part = fixed((normalize(middles[k])[0] * gain_two).astype(BF16))
        hiddens.append(both_pairs(hidden_part))
    hidden_two = (hiddens[0][0], hiddens[1][0], hiddens[0][1], hiddens[1][1])
    middle = fixed(jnp.concatenate(middles, 0))
    normed_two, inverse_two = normalize(middle)
    two_left = left_side(*hidden_two)

    def terms_of(weights):
        terms = hidden_units(ring, hidden_two, grad_low, weights)
        return terms, ring.swap_core(terms)

    def gradient(left, rights):
        sides = ([x[0] for x in left], [x[1] for x in left], rights)
        part = weight_grad(far, *sides)
        sent = ring.swap_pair(part)
        parts = weight_grad(near, *sides, sent, split=True)
        return part, [parts[0]] + [
            ring.shift_group(parts[shift], shift) for shift in range(1, ring.groups)
        ]

    def summed(parts, begin=0, end=None):
        total = parts[0][:, begin:end].astype(F32)
        for part in parts[1:]:
            total = total + part[:, begin:end].astype(F32)
        return total

    def hidden_grads(terms, got):
        lefts = (grad_left, two_left)
        rights = [(0, terms, got, 0), (1, terms, got, 1), (1, terms, got, 2)]
        part = weight_grad(near, [x[0] for x in lefts], [x[1] for x in lefts], rights, whole=True)
        part = lax.psum_scatter(
            part, "dp", scatter_dimension=0, tiled=True, axis_index_groups=ring.group_list()
        )
        return part.reshape(ring.pairs, rows, -1)

    def halves_joined(part):
        mine = lax.dynamic_index_in_dim(part, pair, 0, keepdims=False)
        other = lax.dynamic_index_in_dim(part, 1 - pair, 0, keepdims=False)
        other = ring.swap_pair(other)
        return jnp.where(pair == 0, mine, other), jnp.where(pair == 0, other, mine)

    def pair_sum(low, after=None):
        sent = ring.swap_pair(low[1])
        if after is not None:
            sent = fixed((sent, after))[0]
        return (low[0].astype(F32) + sent.astype(F32)).astype(BF16)

    terms_a, got_a = terms_of(weights_a)
    two_part = back_project(ring, terms_a, (1, 2), weights_a, 0, None, F32)
    grads_a = hidden_grads(terms_a, got_a)
    mlp_part = back_project(ring, terms_a, (0,), weights_a, 2, None, F32)
    terms_b, got_b = terms_of(weights_b)
    two_sums, low = [], None
    for piece in range(2):
        before = low
        low = back_project(ring, terms_b, (1, 2), weights_b, 0, two_part, BF16, piece, 2)
        low = fixed(pair_sum(low, before))
        two_sums.append(tensor_sum(low))
    hidden_two_grad = jnp.concatenate(two_sums, 1)
    grads_b = hidden_grads(terms_b, got_b)
    mlp_low = back_project(ring, terms_b, (0,), weights_b, 2, mlp_part, BF16)
    mlp_low = pair_sum(mlp_low)

    mlp_gain_part = jnp.sum(hidden_two_grad * normed_two, axis=0)
    scaled = hidden_two_grad * gain_two
    middle_grad = out_grad + inverse_two * (
        scaled - normed_two * jnp.mean(scaled * normed_two, axis=-1, keepdims=True)
    )
    middle_grad, middle_low = fixed((middle_grad, middle_grad.astype(BF16)))
    attended_grad = dot(middle_low, out_t, 1, 0, BF16)
    middle_left = left_side(middle_low)
    qkv_back = attention_backward(
        query, keys, value, attended, attended_grad, log_total, cosine, signed_sine,
        segment_ids, kv_heads,
    )
    block_output = middle + tensor_sum(mlp_low, qkv_back)
    qkv_got = ring.swap_core(qkv_back)
    _, out_parts = gradient([middle_left], [(0, attended[None], attended_got[None], 0)])
    far_rows, qkv_parts = gradient([one_left], [(0, qkv_back[None], qkv_got[None], 0)])
    one_low = dot(fixed((qkv_back, far_rows))[0], full_qkv, 1, 1, BF16)
    attn_gain_part = jnp.sum(one_low.astype(F32) * normed_one, axis=0)
    hidden_one_grad = tensor_sum(one_low, attn_gain_part)
    scaled_one = hidden_one_grad * gain_one
    input_grad = middle_grad + inverse_one * (
        scaled_one - normed_one * jnp.mean(scaled_one * normed_one, axis=-1, keepdims=True)
    )

    if ring.tensor == 2:
        other = lax.ppermute(attn_gain_part, "tensor", [(0, 1), (1, 0)])
        attn_gain_part = attn_gain_part + other
    else:
        attn_gain_part = lax.psum(attn_gain_part, "tensor")
    small = jnp.stack([attn_gain_part, mlp_gain_part], 0)
    small = small + ring.swap_core(small)
    small = small + ring.swap_pair(small)
    small = small.reshape(2, ring.groups, ring.pairs, ring.cores, rows)
    small = lax.dynamic_index_in_dim(small, core, 3, keepdims=False)
    small = lax.dynamic_index_in_dim(small, pair, 2, keepdims=False)
    own = lax.dynamic_index_in_dim(small, my_group, 1, keepdims=False)
    for shift in range(1, ring.groups):
        target = (my_group + shift) % ring.groups
        piece = lax.dynamic_index_in_dim(small, target, 1, keepdims=False)
        own = own + ring.shift_group(piece, shift)

    qkv_parts, out_parts, _ = fixed((qkv_parts, out_parts, own))
    joined_a = halves_joined(grads_a)
    joined_b = halves_joined(grads_b)
    size_a, size_b = bounds[0][1] - bounds[0][0], bounds[1][1] - bounds[1][0]

    def assembled(part):
        pieces = []
        for left, right in zip(joined_a, joined_b):
            pieces.append(left[:, part * size_a : (part + 1) * size_a])
            pieces.append(right[:, part * size_b : (part + 1) * size_b])
        return jnp.concatenate(pieces, 1).astype(F32)

    return (
        block_output,
        input_grad,
        own[0],
        summed(qkv_parts, 0, q_cols),
        summed(qkv_parts, q_cols, q_cols + kv_cols),
        summed(qkv_parts, q_cols + kv_cols),
        summed(out_parts).T,
        own[1],
        assembled(1),
        assembled(2),
        assembled(0).T,
    )


def solution(mesh):
    ring = Ring(mesh.shape["dp"], mesh.shape["tensor"])
    rows, line, down, across = P("dp", None), P("dp"), P("dp", "tensor"), P("tensor", "dp")
    ins = (rows, line, line, line, down, down, down, across, line, down, down, across, rows)
    outs = (rows, rows, line, down, down, down, across, line, down, down, across)

    def body(*args):
        return per_device(ring, *args)

    return jax.shard_map(
        body,
        mesh=mesh,
        in_specs=ins,
        out_specs=outs,
        check_vma=False,
    )
```

```python
import functools
import math

import jax
import jax.numpy as jnp
from jax import lax
from jax.experimental import pallas as pl
from jax.experimental.pallas import tpu as pltpu
from jax.sharding import PartitionSpec as P


fixed = lax.optimization_barrier

HEAD_SIZE = 64
EPSILON = 1e-05
MASKED = -1e30
LANES = 128
F32 = jnp.float32
BF16 = jnp.bfloat16


def dot(a, b, ca, cb, out=F32):
    return lax.dot_general(a, b, (((ca,), (cb,)), ((), ())), preferred_element_type=out)


def cost(flops, moved, exps=0):
    return pl.CostEstimate(flops=int(flops), bytes_accessed=int(moved), transcendentals=int(exps))


def params(count=1):
    return pltpu.CompilerParams(
        dimension_semantics=("arbitrary",) * count, vmem_limit_bytes=60 * 1024 * 1024
    )


def normalize(values):
    inverse = lax.rsqrt(jnp.mean(values * values, axis=-1, keepdims=True) + EPSILON)
    return (values * inverse, inverse)


def tile_of(width, most):
    tile = most
    while width % tile:
        tile //= 2
    return tile


class Ring:
    def __init__(self, dp, tensor):
        self.dp, self.tensor, self.width = dp, tensor, None
        self.cores = self.pairs = 2
        self.groups = dp // 4

    def at(self, g, p, c):
        return (g * self.pairs + p) * self.cores + c

    def members(self):
        return [
            (g, p, c)
            for g in range(self.groups)
            for p in range(self.pairs)
            for c in range(self.cores)
        ]

    def move(self, value, where):
        return lax.ppermute(
            value, "dp", [(self.at(*m), self.at(*where(*m))) for m in self.members()]
        )

    def swap_core(self, value):
        return self.move(value, lambda g, p, c: (g, p, 1 - c))

    def swap_pair(self, value):
        return self.move(value, lambda g, p, c: (g, 1 - p, c))

    def shift_group(self, value, shift):
        return self.move(value, lambda g, p, c: ((g + shift) % self.groups, p, c))

    def column_list(self):
        return [
            [self.at(g, p, c) for g in range(self.groups) for c in range(self.cores)]
            for p in range(self.pairs)
        ]

    def group_list(self):
        return [
            [self.at(g, p, c) for g in range(self.groups)]
            for p in range(self.pairs)
            for c in range(self.cores)
        ]


def rotate(values, cosine, signed_sine, lane):
    ahead = pltpu.roll(values, LANES - HEAD_SIZE // 2, 1)
    behind = pltpu.roll(values, HEAD_SIZE // 2, 1)
    crossed = jnp.where(lane % HEAD_SIZE < HEAD_SIZE // 2, ahead, behind)
    return values * cosine + crossed * signed_sine


def twice(values, second, lane):
    other = pltpu.roll(values, HEAD_SIZE, 1)
    low = lane < HEAD_SIZE
    return jnp.where(second, jnp.where(low, other, values), jnp.where(low, values, other))


def attention_forward_kernel(
    per_kv, tile, q_ref, k_ref, v_ref, cos_ref, sin_ref, seg_row, seg_col,
    q_out, k_out, v_out, o_ref, lse_ref, mask,
):
    step = pl.program_id(0)
    tokens = q_ref.shape[0]
    lane = lax.broadcasted_iota(jnp.int32, (tokens, LANES), 1)
    scale = HEAD_SIZE**-0.5

    @pl.when(step == 0)
    def _():
        row = lax.broadcasted_iota(jnp.int32, (tokens, tokens), 0)
        col = lax.broadcasted_iota(jnp.int32, (tokens, tokens), 1)
        allowed = (seg_col[...] == seg_row[...]) & (col <= row)
        mask[...] = jnp.where(allowed, 0.0, MASKED)
        k_out[...] = rotate(k_ref[...], cos_ref[...], sin_ref[...], lane).astype(BF16)
        v_out[...] = v_ref[...].astype(BF16)
        lse_ref[...] = jnp.zeros_like(lse_ref)

    second = step // per_kv == 1
    low = lane < HEAD_SIZE
    query = rotate(q_ref[...], cos_ref[...], sin_ref[...], lane)
    q_out[...] = query.astype(BF16)
    keys = twice(k_out[...].astype(F32), second, lane).astype(BF16)
    value = twice(v_out[...].astype(F32), second, lane)
    for start in range(0, tokens, tile):
        seen = start + tile
        total = jnp.zeros((tile, LANES), F32)
        for half in range(2):
            inside = low if half == 0 else ~low
            part = jnp.where(inside[:tile], query[start:seen], 0.0).astype(BF16)
            scores = dot(part, keys[:seen], 1, 1) * scale + mask[start:seen, :seen]
            peak = jnp.max(scores, axis=1, keepdims=True)
            weights = jnp.exp(scores - peak)
            norm = jnp.sum(weights, axis=1, keepdims=True)
            probability = (weights / norm).astype(BF16)
            shown = jnp.where(inside, value, 0.0).astype(BF16)
            total += dot(probability, shown[:seen], 1, 0)
            log_total = peak + jnp.log(norm)
            here = lane[:tile] == 2 * step + half
            lse_ref[start:seen, :] = jnp.where(here, log_total, lse_ref[start:seen, :])
        o_ref[start:seen, :] = total.astype(BF16)


def attention_forward(qkv, cosine, signed_sine, segments, heads, kv_heads):
    tokens = qkv.shape[0]
    steps = heads // 2
    tile = tile_of(tokens, 256)
    fixed = lambda j: (0, 0)
    block = (tokens, LANES)
    scores = heads * tokens * tokens
    return pl.pallas_call(
        functools.partial(attention_forward_kernel, steps // kv_heads, tile),
        grid=(steps,),
        in_specs=[
            pl.BlockSpec(block, lambda j: (0, j)),
            pl.BlockSpec(block, lambda j: (0, steps)),
            pl.BlockSpec(block, lambda j: (0, steps + 1)),
            pl.BlockSpec(block, fixed),
            pl.BlockSpec(block, fixed),
            pl.BlockSpec((1, tokens), fixed),
            pl.BlockSpec((tokens, 1), fixed),
        ],
        out_specs=[
            pl.BlockSpec(block, lambda j: (0, j)),
            pl.BlockSpec(block, fixed),
            pl.BlockSpec(block, fixed),
            pl.BlockSpec(block, lambda j: (0, j)),
            pl.BlockSpec(block, fixed),
        ],
        out_shape=[
            jax.ShapeDtypeStruct((tokens, heads * HEAD_SIZE), BF16),
            jax.ShapeDtypeStruct(block, BF16),
            jax.ShapeDtypeStruct(block, BF16),
            jax.ShapeDtypeStruct((tokens, heads * HEAD_SIZE), BF16),
            jax.ShapeDtypeStruct(block, F32),
        ],
        scratch_shapes=[pltpu.VMEM((tokens, tokens), F32)],
        compiler_params=params(),
        cost_estimate=cost(4 * scores * HEAD_SIZE, 6 * tokens * qkv.shape[1], scores),
        name="attention_forward",
    )(qkv, qkv, qkv, cosine, signed_sine, segments[None, :], segments[:, None])


def attention_backward_kernel(
    part, steps, tile, q_ref, k_ref, v_ref, o_ref, do_ref, lse_ref, cos_ref, sin_ref,
    seg_row, seg_col, *refs,
):
    if part:
        key_before, value_before, out_ref, mask, key_part, value_part = refs
    else:
        out_ref, key_out, value_out, mask, key_part, value_part = refs
    step = pl.program_id(0)
    tokens = q_ref.shape[0]
    lane = lax.broadcasted_iota(jnp.int32, (tokens, LANES), 1)
    low = lane < HEAD_SIZE
    scale = HEAD_SIZE**-0.5

    @pl.when(step == 0)
    def _():
        row = lax.broadcasted_iota(jnp.int32, (tokens, tokens), 0)
        col = lax.broadcasted_iota(jnp.int32, (tokens, tokens), 1)
        allowed = (seg_col[...] == seg_row[...]) & (col <= row)
        mask[...] = jnp.where(allowed, 0.0, MASKED)
        key_part[...] = jnp.zeros_like(key_part)
        value_part[...] = jnp.zeros_like(value_part)

    @pl.when(step < steps)
    def _():
        keys = twice(k_ref[...].astype(F32), part == 1, lane)
        value = twice(v_ref[...].astype(F32), part == 1, lane).astype(BF16)
        keys_low = keys.astype(BF16)
        given = do_ref[...].astype(F32)
        product = given * o_ref[...].astype(F32)
        query = q_ref[...].astype(F32)
        for start in range(0, tokens, tile):
            seen = start + tile
            total = jnp.zeros((tile, LANES), F32)
            for half in range(2):
                inside = low if half == 0 else ~low
                near = inside[:tile]
                part_q = jnp.where(near, query[start:seen], 0.0).astype(BF16)
                grad = jnp.where(near, given[start:seen], 0.0).astype(BF16)
                terms = jnp.sum(
                    jnp.where(near, product[start:seen], 0.0), axis=1, keepdims=True
                )
                here = lane[:tile] == 2 * (step + part * steps) + half
                log_total = jnp.sum(
                    jnp.where(here, lse_ref[start:seen, :], 0.0), axis=1, keepdims=True
                )
                scores = dot(part_q, keys_low[:seen], 1, 1) * scale + mask[start:seen, :seen]
                weights = jnp.exp(scores - log_total)
                slope = dot(grad, value[:seen], 1, 1)
                back = (weights * (slope - terms)).astype(BF16)
                shown = jnp.where(inside, keys, 0.0).astype(BF16)
                total += dot(back, shown[:seen], 1, 0)
                key_part[:seen, :] += dot(back, part_q, 0, 0)
                value_part[:seen, :] += dot(weights.astype(BF16), grad, 0, 0)
            out_ref[start:seen, :] = rotate(
                total * scale, cos_ref[start:seen, :], -sin_ref[start:seen, :], lane[:tile]
            ).astype(BF16)

    def folded(sums):
        return sums[...] + pltpu.roll(sums[...], HEAD_SIZE, 1)

    if part == 0:

        @pl.when(step == steps - 1)
        def _():
            key_out[...] = folded(key_part)
            value_out[...] = folded(value_part)

    else:

        @pl.when(step == steps)
        def _():
            total = jnp.where(low, key_before[...], folded(key_part))
            out_ref[...] = rotate(
                total * scale, cos_ref[...], -sin_ref[...], lane
            ).astype(BF16)

        @pl.when(step == steps + 1)
        def _():
            out_ref[...] = jnp.where(low, value_before[...], folded(value_part)).astype(BF16)


def attention_backward(
    part, before, query, keys, value, attended, attended_grad, log_total, cosine, signed_sine,
    segments,
):
    tokens, width = query.shape
    steps = width // LANES // 2
    tile = tile_of(tokens, 256)
    fixed_block = lambda j: (0, 0)
    moving = lambda j: (0, part * steps + jnp.minimum(j, steps - 1))
    block = (tokens, LANES)
    scores = width // HEAD_SIZE * tokens * tokens // 2
    outs = pl.BlockSpec(block, lambda j: (0, j))
    shapes = jax.ShapeDtypeStruct((tokens, (steps + 2 * part) * LANES), BF16)
    if part == 0:
        outs = [outs] + [pl.BlockSpec(block, fixed_block)] * 2
        shapes = [shapes] + [jax.ShapeDtypeStruct(block, F32)] * 2
    return pl.pallas_call(
        functools.partial(attention_backward_kernel, part, steps, tile),
        grid=(steps + 2 * part,),
        in_specs=[
            pl.BlockSpec(block, moving),
            pl.BlockSpec(block, fixed_block),
            pl.BlockSpec(block, fixed_block),
            pl.BlockSpec(block, moving),
            pl.BlockSpec(block, moving),
            pl.BlockSpec(block, fixed_block),
            pl.BlockSpec(block, fixed_block),
            pl.BlockSpec(block, fixed_block),
            pl.BlockSpec((1, tokens), fixed_block),
            pl.BlockSpec((tokens, 1), fixed_block),
        ]
        + [pl.BlockSpec(block, fixed_block)] * len(before),
        out_specs=outs,
        out_shape=shapes,
        scratch_shapes=[pltpu.VMEM((tokens, tokens), F32)] + [pltpu.VMEM(block, F32)] * 2,
        compiler_params=params(),
        cost_estimate=cost(10 * scores * HEAD_SIZE, 4 * tokens * width, scores),
        name="attention_backward",
    )(
        query, keys, value, attended, attended_grad, log_total, cosine, signed_sine,
        segments[None, :], segments[:, None], *before,
    )


def gathered_order(ring, width):
    rows = ring.width // ring.dp
    block = ring.pairs * ring.cores
    places = []
    for begin in range(0, width // rows, block):
        for p in range(ring.pairs):
            for c in range(ring.cores):
                places.append((begin + p * ring.cores + c, begin + c * ring.pairs + p))
    return [(slice(a * rows, (a + 1) * rows), slice(b * rows, (b + 1) * rows)) for a, b in places]


def hidden_kernel(ring, pieces, *refs):
    gate_ref, up_ref, down_ref, out, hidden, given = refs[pieces:]

    @pl.when(pl.program_id(0) == 0)
    def _():
        for held, parts in ((hidden, refs[: pieces - 2]), (given, refs[pieces - 2 : pieces])):
            at = 0
            for part in parts:
                for place, found in gathered_order(ring, part.shape[1]):
                    held[at : at + part.shape[0], found] = part[:, place]
                at += part.shape[0]

    for begin in range(0, out.shape[2], 256):
        here = slice(begin, min(begin + 256, out.shape[2]))
        gate = dot(hidden[...], gate_ref[:, here], 1, 0)
        up = dot(hidden[...], up_ref[:, here], 1, 0)
        grad = dot(given[...], down_ref[:, here], 1, 0)
        sigma = jax.nn.sigmoid(gate)
        swish = gate * sigma
        out[0, :, here] = (swish * up).astype(BF16)
        out[1, :, here] = (grad * up * sigma * (1.0 + gate * (1.0 - sigma))).astype(BF16)
        out[2, :, here] = (grad * swish).astype(BF16)


def hidden_units(ring, hidden_two, grad_low, weights):
    tokens, width = sum(part.shape[0] for part in grad_low), weights.shape[0]
    units = weights.shape[-1] // 3
    tile = 256 if units % 256 == 0 else units
    count = units // tile
    pieces = [*hidden_two, *grad_low]

    def columns(part):
        buffers = pl.Buffered(1 if count == 1 else 2)
        return pl.BlockSpec(
            (width, tile), lambda j: (0, part * count + j), pipeline_mode=buffers
        )

    return pl.pallas_call(
        functools.partial(hidden_kernel, ring, len(pieces)),
        grid=(count,),
        in_specs=[
            pl.BlockSpec(part.shape, lambda j: (0, 0), pipeline_mode=pl.Buffered(1))
            for part in pieces
        ]
        + [columns(0), columns(1), columns(2)],
        out_specs=pl.BlockSpec((3, tokens, tile), lambda j: (0, 0, j)),
        out_shape=jax.ShapeDtypeStruct((3, tokens, units), BF16),
        scratch_shapes=[pltpu.VMEM((tokens, width), BF16)] * 2,
        compiler_params=params(),
        cost_estimate=cost(6 * tokens * width * units, 6 * width * units, tokens * units),
        name="hidden_units",
    )(*pieces, weights, weights, weights)


def back_kernel(ring, parts, has_start, *refs):
    values, weights = refs[:parts], refs[parts : 2 * parts]
    total = dot(values[0][...], weights[0][...], 1, 1)
    for value, weight in zip(values[1:], weights[1:]):
        total += dot(value[...], weight[...], 1, 1)
    tokens = refs[-1].shape[0]
    for at, out in ((0, refs[-2]), (1, refs[-1])):
        for place, found in gathered_order(ring, out.shape[1]):
            part = total[at * tokens : (at + 1) * tokens, found]
            if has_start:
                part += refs[2 * parts + at][:, place].astype(F32)
            out[:, place] = part.astype(out.dtype)


def back_project(ring, terms, start=None, piece=0, pieces=1):
    both = terms[0][0].shape[1]
    tokens = both // 2
    width = terms[0][2].shape[0]
    tile = min(512, width // pieces)
    count = width // pieces // tile

    def chosen(pick, units):
        return pl.BlockSpec((None, both, units), lambda j: (pick, 0, 0))

    def columns(part, units):
        return pl.BlockSpec((tile, units), lambda j: (piece * count + j, part))

    sizes = [values.shape[2] for values, _, _, _ in terms]
    begin = pl.BlockSpec((tokens, tile), lambda j: (0, piece * count + j))
    return pl.pallas_call(
        functools.partial(back_kernel, ring, len(terms), start is not None),
        grid=(count,),
        in_specs=[chosen(pick, units) for (_, pick, _, _), units in zip(terms, sizes)]
        + [columns(part, units) for (_, _, _, part), units in zip(terms, sizes)]
        + ([begin] * 2 if start is not None else []),
        out_specs=[pl.BlockSpec((tokens, tile), lambda j: (0, j))] * 2,
        out_shape=[jax.ShapeDtypeStruct((tokens, count * tile), BF16)] * 2,
        compiler_params=params(),
        cost_estimate=cost(
            2 * both * width * sum(sizes) // pieces, 2 * width * sum(sizes) // pieces
        ),
        name="back_project",
    )(
        *(values for values, _, _, _ in terms),
        *(weights for _, _, weights, _ in terms),
        *(start if start is not None else ()),
    )


def transpose_kernel(*refs):
    refs[-1][...] = jnp.concatenate([ref[...] for ref in refs[:-1]], 0).T


def transposed(values):
    tokens, width = values[0].shape
    tile = tile_of(width, 512)
    count = len(values)
    return pl.pallas_call(
        transpose_kernel,
        grid=(width // tile,),
        in_specs=[pl.BlockSpec((tokens, tile), lambda j: (0, j))] * count,
        out_specs=pl.BlockSpec((tile, count * tokens), lambda j: (j, 0)),
        out_shape=jax.ShapeDtypeStruct((width, count * tokens), values[0].dtype),
        compiler_params=params(),
        cost_estimate=cost(0, 4 * tokens * width * count),
        name="transposed",
    )(*values)


def grad_kernel(layout, lefts, rights, has_extra, pieces, where, *refs):
    own_left, got_left = refs[:lefts], refs[lefts : 2 * lefts]
    own_right = refs[2 * lefts : 2 * lefts + rights]
    got_right = refs[2 * lefts + rights : 2 * lefts + 2 * rights]
    step = pl.program_id(0)
    rows, tokens = own_left[0].shape[-2:]
    height = own_left[0].shape[0] * own_left[0].shape[1] * rows
    for left, right, begin, end in layout:

        @pl.when((step >= begin) & (step < end))
        def _():
            shape = (height, tokens)
            total = dot(own_left[left][...].reshape(shape), own_right[right][...], 1, 0)
            total += dot(got_left[left][...].reshape(shape), got_right[right][...], 1, 0)
            if has_extra:
                total += refs[2 * lefts + 2 * rights][...].astype(F32)
            if pieces == 0:
                refs[-1][...] = total.astype(BF16)
                return
            outs, held = refs[-pieces - 1 : -1], refs[-1]
            held[...] = total
            for shift, out in enumerate(outs):
                start = pl.multiple_of(where[2 + shift] * rows, rows)
                out[...] = held[pl.ds(start, rows), :].astype(BF16)


def weight_grad(where, own_left, got_left, rights, extra=None, split=False, whole=False):
    groups, pairs, _, rows, tokens = own_left[0].shape
    taken = pairs if whole else 1
    height = groups * taken * rows
    tile = math.gcd(*(own.shape[-1] for _, own, _, _ in rights))
    tile //= next(n for n in range(1, tile) if tile // n <= (1024 if whole else 1536) and tile % (n * LANES) == 0)
    layout, columns, begin = [], [], 0
    for k, (left, own, _, pick) in enumerate(rights):
        count = own.shape[-1] // tile
        layout.append((left, k, begin, begin + count))
        columns.append(
            pl.BlockSpec(
                (None, tokens, tile),
                functools.partial(
                    lambda j, w, p, b, n: (p, 0, jnp.clip(j - b, 0, n - 1)),
                    p=pick,
                    b=begin,
                    n=count,
                ),
            )
        )
        begin += count
    own = pl.BlockSpec(
        (groups, taken, 1, rows, tokens), lambda j, w: (0, 0 if whole else w[0], w[1], 0, 0)
    )
    got = pl.BlockSpec(
        (groups, taken, rows, tokens), lambda j, w: (0, 0 if whole else w[0], 0, 0)
    )
    out = pl.BlockSpec((height, tile), lambda j, w: (0, j))
    args = [*own_left, *got_left, *(r[1] for r in rights), *(r[2] for r in rights)]
    specs = [own] * len(own_left) + [got] * len(got_left) + columns * 2
    shapes = jax.ShapeDtypeStruct((height, begin * tile), BF16)
    outs, scratch, pieces = out, [], 0
    if extra is not None:
        args.append(extra)
        specs.append(out)
    if split:
        pieces = groups
        outs = [pl.BlockSpec((rows, tile), lambda j, w: (0, j))] * groups
        shapes = [jax.ShapeDtypeStruct((rows, begin * tile), BF16)] * groups
        scratch = [pltpu.VMEM((height, tile), F32)]
    return pl.pallas_call(
        functools.partial(
            grad_kernel, tuple(layout), len(own_left), len(rights), extra is not None, pieces
        ),
        grid_spec=pltpu.PrefetchScalarGridSpec(
            num_scalar_prefetch=1,
            grid=(begin,),
            in_specs=specs,
            out_specs=outs,
            scratch_shapes=scratch,
        ),
        out_shape=shapes,
        compiler_params=params(),
        cost_estimate=cost(
            4 * height * tokens * begin * tile, 2 * (height + 2 * tokens) * begin * tile
        ),
        name="weight_grad",
    )(where, *args)


def middle_kernel(parts, *refs):
    middle, given, gain = refs[2 * parts : 2 * parts + 3]
    grad_out, low_out, turned_out, sums_out = refs[2 * parts + 3 :]
    total = jnp.concatenate(
        [refs[k][...].astype(F32) + refs[parts + k][...].astype(F32) for k in range(parts)], 1
    )
    normed, inverse = normalize(middle[...])

    @pl.when(pl.program_id(0) == 0)
    def _():
        sums_out[...] = jnp.zeros_like(sums_out)

    sums_out[...] += jnp.sum(total * normed, axis=0, keepdims=True)
    scaled = total * gain[...]
    grad = given[...] + inverse * (
        scaled - normed * jnp.mean(scaled * normed, axis=-1, keepdims=True)
    )
    grad_out[...] = grad
    low_out[...] = grad.astype(BF16)
    turned_out[...] = grad.astype(BF16).T


def middle_backward(own, other, middle, out_grad, gain):
    tokens, width = middle.shape
    tile = 128
    rows = pl.BlockSpec((tile, width), lambda i: (i, 0))
    line = pl.BlockSpec((1, width), lambda i: (0, 0))
    pieces = [pl.BlockSpec((tile, part.shape[1]), lambda i: (i, 0)) for part in own]
    return pl.pallas_call(
        functools.partial(middle_kernel, len(own)),
        grid=(tokens // tile,),
        in_specs=pieces * 2 + [rows, rows, line],
        out_specs=[rows, rows, pl.BlockSpec((width, tile), lambda i: (0, i)), line],
        out_shape=[
            jax.ShapeDtypeStruct((tokens, width), F32),
            jax.ShapeDtypeStruct((tokens, width), BF16),
            jax.ShapeDtypeStruct((width, tokens), BF16),
            jax.ShapeDtypeStruct((1, width), F32),
        ],
        compiler_params=params(),
        cost_estimate=cost(20 * tokens * width, 20 * tokens * width),
        name="middle_backward",
    )(*own, *other, middle, out_grad, gain[None])


def input_kernel(own, other, block_input, grad, gain, out):
    total = own[...].astype(F32) + other[...].astype(F32)
    normed, inverse = normalize(block_input[...].astype(F32))
    scaled = total * gain[...]
    out[...] = grad[...] + inverse * (
        scaled - normed * jnp.mean(scaled * normed, axis=-1, keepdims=True)
    )


def input_backward(own, other, block_input, middle_grad, gain):
    tokens, width = middle_grad.shape
    rows = pl.BlockSpec((128, width), lambda i: (i, 0))
    return pl.pallas_call(
        input_kernel,
        grid=(tokens // 128,),
        in_specs=[rows] * 4 + [pl.BlockSpec((1, width), lambda i: (0, 0))],
        out_specs=rows,
        out_shape=jax.ShapeDtypeStruct((tokens, width), F32),
        compiler_params=params(),
        cost_estimate=cost(10 * tokens * width, 14 * tokens * width),
        name="input_backward",
    )(own, other, block_input, middle_grad, gain[None])


def joined_kernel(sizes, half, pair, *refs):
    mine, sent, (gate, up, down) = refs[: len(sizes)], refs[len(sizes) : -3], refs[-3:]
    for index in range(2):
        begin = index * half
        for own, other, size in zip(mine, sent, sizes):
            part = jnp.where(pair[0] == index, own[...].astype(F32), other[...].astype(F32))
            down[begin : begin + size, :] = part[:, :size].T
            gate[:, begin : begin + size] = part[:, size : 2 * size]
            up[:, begin : begin + size] = part[:, 2 * size :]
            begin += size


def joined(pair, mine, sent):
    rows = sent[0].shape[0]
    sizes = [part.shape[1] // 3 for part in sent]
    half = sum(sizes)
    wide = jax.ShapeDtypeStruct((rows, 2 * half), F32)
    return pl.pallas_call(
        functools.partial(joined_kernel, sizes, half),
        grid_spec=pltpu.PrefetchScalarGridSpec(
            num_scalar_prefetch=1,
            grid=(1,),
            in_specs=[
                pl.BlockSpec((None, *part.shape[1:]), lambda i, p: (p[0], 0, 0)) for part in mine
            ]
            + [pl.BlockSpec(part.shape, lambda i, p: (0, 0)) for part in sent],
            out_specs=[
                pl.BlockSpec((rows, 2 * half), lambda i, p: (0, 0)),
                pl.BlockSpec((rows, 2 * half), lambda i, p: (0, 0)),
                pl.BlockSpec((2 * half, rows), lambda i, p: (0, 0)),
            ],
        ),
        out_shape=[wide, wide, jax.ShapeDtypeStruct((2 * half, rows), F32)],
        compiler_params=params(),
        cost_estimate=cost(0, 40 * rows * half),
        name="joined",
    )(pair, *mine, *sent)


def per_device(
    ring,
    block_input,
    segment_ids,
    position_ids,
    attn_gain,
    w_query,
    key_projection_weight,
    value_projection_weight,
    w_out,
    mlp_gain,
    w_gate,
    w_up,
    w_down,
    out_grad,
):
    seq_len, width = block_input.shape
    ring.width = width
    rows = w_query.shape[0]
    q_cols, kv_cols = w_query.shape[1], key_projection_weight.shape[1]
    heads, kv_heads = q_cols // HEAD_SIZE, kv_cols // HEAD_SIZE
    hidden = w_gate.shape[1]
    me = lax.axis_index("dp")
    core = me % ring.cores
    pair = (me // ring.cores) % ring.pairs
    my_group = me // (ring.cores * ring.pairs)

    def swap_tensor(low):
        return lax.ppermute(low, "tensor", [(0, 1), (1, 0)])

    def tensor_sum(low, after=None):
        other = swap_tensor(low)
        if after is not None:
            other = fixed((other, after))[0]
        return low.astype(F32) + other.astype(F32)

    gains = jnp.pad(jnp.stack([attn_gain, mlp_gain], 1), ((0, 0), (0, LANES - 2)))
    qkv_cols = q_cols + 2 * kv_cols
    first = lax.all_gather(
        jnp.concatenate(
            [w_query, key_projection_weight, value_projection_weight, w_out.T, gains], 1
        ),
        "dp",
        axis=0,
        tiled=True,
    )
    half = hidden // ring.pairs
    cut = (half // LANES * 6 // 11) * LANES
    bounds = ((0, cut), (cut, half))
    local = jnp.stack([w_gate, w_up, w_down.T], 1).reshape(rows, 3, ring.pairs, half)

    def of_pair(index):
        return lax.dynamic_index_in_dim(local, index, 2, keepdims=False)

    kept = of_pair(pair)
    sent = ring.swap_pair(of_pair(1 - pair))
    both = jnp.stack([jnp.where(pair == 0, kept, sent), jnp.where(pair == 0, sent, kept)], 0)
    weights_a, weights_b = [
        lax.all_gather(
            both[..., a:b].reshape(ring.pairs * rows, 3 * (b - a)),
            "dp",
            axis=0,
            tiled=True,
            axis_index_groups=ring.column_list(),
        )
        for a, b in bounds
    ]
    full_qkv = first[:, :qkv_cols]
    out_t = first[:, qkv_cols : qkv_cols + w_out.shape[0]]
    gain_rows = first[:, qkv_cols + w_out.shape[0] :].T.astype(F32)
    gain_one, gain_two = gain_rows[0], gain_rows[1]

    def left_side(*values):
        return left_rows(transposed(values))

    def left_rows(turned):
        own = turned.reshape(ring.groups, ring.pairs, ring.cores, rows, -1)
        give = lax.dynamic_index_in_dim(own, 1 - core, 2, keepdims=False)
        return own, ring.swap_core(give)

    targets = [(my_group + shift) % ring.groups for shift in range(ring.groups)]
    far = jnp.stack([1 - pair, core, *targets]).astype(jnp.int32)
    near = jnp.stack([pair, core, *targets]).astype(jnp.int32)

    residual_in = block_input.astype(F32)
    normed_one, _ = normalize(residual_in)
    hidden_one = fixed((normed_one * gain_one).astype(BF16))
    half_dim = HEAD_SIZE // 2
    frequency = 10000.0 ** (-(jnp.arange(half_dim, dtype=F32) * 2.0 / HEAD_SIZE))
    angles = position_ids.astype(F32)[:, None] * frequency[None, :]
    cosine, sine = jnp.cos(angles), jnp.sin(angles)
    cosine = jnp.concatenate([cosine] * 4, 1)
    signed_sine = jnp.concatenate([-sine, sine, -sine, sine], 1)
    qkv = dot(hidden_one, full_qkv, 1, 0)

    def both_pairs(values):
        return values, ring.swap_pair(values)

    grad_low = both_pairs(fixed((out_grad.astype(BF16), qkv))[0])
    grad_left = left_side(*grad_low)
    query, keys, value, attended, log_total = attention_forward(
        qkv, cosine, signed_sine, segment_ids, heads, kv_heads
    )
    attended_got = ring.swap_core(attended)
    one_left = left_side(hidden_one)
    middles, hiddens = [], []
    for k in range(2):
        part = slice(k * seq_len // 2, (k + 1) * seq_len // 2)
        low = dot(attended[part], out_t, 1, 1, BF16)
        middles.append(residual_in[part] + tensor_sum(low, hiddens[-1][0] if k else None))
        hidden_part = fixed((normalize(middles[k])[0] * gain_two).astype(BF16))
        hiddens.append(both_pairs(hidden_part))
    hidden_two = (hiddens[0][0], hiddens[1][0], hiddens[0][1], hiddens[1][1])
    middle = fixed(jnp.concatenate(middles, 0))
    two_left = left_side(*hidden_two)

    def terms_of(weights):
        terms = hidden_units(ring, hidden_two, grad_low, weights)
        return terms, ring.swap_core(terms)

    def group_sum(part):
        return lax.psum_scatter(
            part, "dp", scatter_dimension=0, tiled=True, axis_index_groups=ring.group_list()
        )

    def gradient(left, rights, direct):
        sides = ([x[0] for x in left], [x[1] for x in left], rights)
        part = weight_grad(far, *sides)
        sent = ring.swap_pair(part)
        parts = weight_grad(near, *sides, sent, split=direct)
        if not direct:
            return part, [group_sum(parts)]
        return part, [parts[0]] + [
            ring.shift_group(parts[shift], shift) for shift in range(1, ring.groups)
        ]

    def summed(parts, begin=0, end=None):
        total = parts[0][:, begin:end].astype(F32)
        for part in parts[1:]:
            total = total + part[:, begin:end].astype(F32)
        return total

    def hidden_grads(terms, got):
        lefts = (grad_left, two_left)
        rights = [(0, terms, got, 0), (1, terms, got, 1), (1, terms, got, 2)]
        part = weight_grad(near, [x[0] for x in lefts], [x[1] for x in lefts], rights, whole=True)
        part = group_sum(part)
        return part.reshape(ring.pairs, rows, -1)

    def for_pair(part):
        other = lax.dynamic_index_in_dim(part, 1 - pair, 0, keepdims=False)
        return ring.swap_pair(other)

    def pair_sum(low, after=None):
        sent = ring.swap_pair(low[1])
        if after is not None:
            sent = fixed((sent, after))[0]
        return (low[0].astype(F32) + sent.astype(F32)).astype(BF16)

    terms_a, got_a = terms_of(weights_a)
    two_part = back_project(ring, [(terms_a, 1, weights_a, 0), (terms_a, 2, weights_a, 1)])
    grads_a = hidden_grads(terms_a, got_a)
    terms_b, got_b = terms_of(weights_b)
    two_own, two_other, low = [], [], None
    for piece in range(PIECES):
        before = low
        low = back_project(
            ring,
            [(terms_b, 1, weights_b, 0), (terms_b, 2, weights_b, 1)],
            two_part,
            piece,
            PIECES,
        )
        low = fixed(pair_sum(low, before))
        two_own.append(low)
        two_other.append(swap_tensor(low))
    grads_b = hidden_grads(terms_b, got_b)
    mlp_low = back_project(ring, [(terms_a, 0, weights_a, 2), (terms_b, 0, weights_b, 2)])
    mlp_low = pair_sum(mlp_low)

    middle_grad, middle_low, middle_turned, mlp_gain_part = middle_backward(
        two_own, two_other, middle, out_grad, gain_two
    )
    attended_grad = dot(middle_low, out_t, 1, 0, BF16)
    middle_left = left_rows(middle_turned)
    qkv_back, qkv_got, before = [], [], ()
    for part in range(2):
        back, *before = jax.tree.leaves(
            attention_backward(
                part, before, query, keys, value, attended, attended_grad, log_total,
                cosine, signed_sine, segment_ids,
            )
        )
        qkv_back.append(back)
        qkv_got.append(ring.swap_core(back))
    block_output = middle + tensor_sum(mlp_low, qkv_back[1])
    rights = [(0, attended[None], attended_got[None], 0)]
    _, out_parts = gradient([middle_left], rights, False)
    qkv_parts = []
    far_rows = []
    for part, (back, got) in enumerate(zip(qkv_back, qkv_got)):
        rights = [(0, back[None], got[None], 0)]
        far_part, parts = gradient([one_left], rights, True)
        far_rows.append(far_part)
        qkv_parts.append(parts)
    qkv_back = jnp.concatenate(qkv_back, 1)
    one_low = dot(fixed((qkv_back, far_rows[0]))[0], full_qkv, 1, 1, BF16)
    attn_gain_part = jnp.sum(one_low.astype(F32) * normed_one, axis=0)
    one_other = swap_tensor(one_low)
    one_other = fixed((one_other, attn_gain_part, block_output))[0]
    input_grad = input_backward(one_low, one_other, block_input, middle_grad, gain_one)

    other = fixed((swap_tensor(attn_gain_part), qkv_parts[1][0]))[0]
    attn_gain_part = attn_gain_part + other
    small = jnp.stack([attn_gain_part, mlp_gain_part[0]], 0)
    small = small + ring.swap_core(small)
    small = small + ring.swap_pair(small)
    small = small.reshape(2, ring.groups, ring.pairs, ring.cores, rows)
    small = lax.dynamic_index_in_dim(small, core, 3, keepdims=False)
    small = lax.dynamic_index_in_dim(small, pair, 2, keepdims=False)
    own = lax.dynamic_index_in_dim(small, my_group, 1, keepdims=False)
    for shift in range(1, ring.groups):
        target = (my_group + shift) % ring.groups
        piece = lax.dynamic_index_in_dim(small, target, 1, keepdims=False)
        own = own + ring.shift_group(piece, shift)

    qkv_parts, out_parts, _ = fixed((qkv_parts, out_parts, own))
    sent = [for_pair(grads_a), for_pair(grads_b)]
    gate_grad, up_grad, down_grad = joined(pair[None], [grads_a, grads_b], sent)

    return (
        block_output,
        input_grad,
        own[0],
        jnp.concatenate([summed(qkv_parts[0]), summed(qkv_parts[1], 0, q_cols // 2)], 1),
        summed(qkv_parts[1], q_cols // 2, q_cols // 2 + kv_cols),
        summed(qkv_parts[1], q_cols // 2 + kv_cols),
        summed(out_parts).T,
        own[1],
        gate_grad,
        up_grad,
        down_grad,
    )


PIECES = 4


def solution(mesh):
    ring = Ring(mesh.shape["dp"], mesh.shape["tensor"])
    rows, line, down, across = P("dp", None), P("dp"), P("dp", "tensor"), P("tensor", "dp")
    ins = (rows, line, line, line, down, down, down, across, line, down, down, across, rows)
    outs = (rows, rows, line, down, down, down, across, line, down, down, across)

    def body(*args):
        return per_device(ring, *args)

    return jax.shard_map(
        body,
        mesh=mesh,
        in_specs=ins,
        out_specs=outs,
        check_vma=False,
    )
```

```python
import functools
import math

import jax
import jax.numpy as jnp
from jax import lax
from jax.experimental import pallas as pl
from jax.experimental.pallas import tpu as pltpu
from jax.sharding import PartitionSpec as P


fixed = lax.optimization_barrier

HEAD_SIZE = 64
EPSILON = 1e-05
MASKED = -1e30
LANES = 128
F32 = jnp.float32
BF16 = jnp.bfloat16


def dot(a, b, ca, cb, out=F32):
    return lax.dot_general(a, b, (((ca,), (cb,)), ((), ())), preferred_element_type=out)


def cost(flops, moved, exps=0):
    return pl.CostEstimate(flops=int(flops), bytes_accessed=int(moved), transcendentals=int(exps))


def params(count=1):
    return pltpu.CompilerParams(
        dimension_semantics=("arbitrary",) * count, vmem_limit_bytes=60 * 1024 * 1024
    )


def normalize(values):
    inverse = lax.rsqrt(jnp.mean(values * values, axis=-1, keepdims=True) + EPSILON)
    return (values * inverse, inverse)


def tile_of(width, most):
    tile = most
    while width % tile:
        tile //= 2
    return tile


class Ring:
    def __init__(self, dp, tensor):
        self.dp, self.tensor, self.width = dp, tensor, None
        self.cores = self.pairs = 2
        self.groups = dp // 4

    def at(self, g, p, c):
        return (g * self.pairs + p) * self.cores + c

    def members(self):
        return [
            (g, p, c)
            for g in range(self.groups)
            for p in range(self.pairs)
            for c in range(self.cores)
        ]

    def move(self, value, where):
        return lax.ppermute(
            value, "dp", [(self.at(*m), self.at(*where(*m))) for m in self.members()]
        )

    def swap_core(self, value):
        return self.move(value, lambda g, p, c: (g, p, 1 - c))

    def swap_pair(self, value):
        return self.move(value, lambda g, p, c: (g, 1 - p, c))

    def shift_group(self, value, shift):
        return self.move(value, lambda g, p, c: ((g + shift) % self.groups, p, c))

    def column_list(self):
        return [
            [self.at(g, p, c) for g in range(self.groups) for c in range(self.cores)]
            for p in range(self.pairs)
        ]

    def group_list(self):
        return [
            [self.at(g, p, c) for g in range(self.groups)]
            for p in range(self.pairs)
            for c in range(self.cores)
        ]


def rotate(values, cosine, signed_sine, lane):
    ahead = pltpu.roll(values, LANES - HEAD_SIZE // 2, 1)
    behind = pltpu.roll(values, HEAD_SIZE // 2, 1)
    crossed = jnp.where(lane % HEAD_SIZE < HEAD_SIZE // 2, ahead, behind)
    return values * cosine + crossed * signed_sine


def twice(values, second, lane):
    other = pltpu.roll(values, HEAD_SIZE, 1)
    low = lane < HEAD_SIZE
    return jnp.where(second, jnp.where(low, other, values), jnp.where(low, values, other))


def attention_forward_kernel(
    per_kv, tile, q_ref, k_ref, v_ref, cos_ref, sin_ref, seg_row, seg_col,
    q_out, k_out, v_out, o_ref, lse_ref, mask,
):
    step = pl.program_id(0)
    tokens = q_ref.shape[0]
    lane = lax.broadcasted_iota(jnp.int32, (tokens, LANES), 1)
    scale = HEAD_SIZE**-0.5

    @pl.when(step == 0)
    def _():
        row = lax.broadcasted_iota(jnp.int32, (tokens, tokens), 0)
        col = lax.broadcasted_iota(jnp.int32, (tokens, tokens), 1)
        allowed = (seg_col[...] == seg_row[...]) & (col <= row)
        mask[...] = jnp.where(allowed, 0.0, MASKED)
        k_out[...] = rotate(k_ref[...], cos_ref[...], sin_ref[...], lane).astype(BF16)
        v_out[...] = v_ref[...].astype(BF16)
        lse_ref[...] = jnp.zeros_like(lse_ref)

    second = step // per_kv == 1
    low = lane < HEAD_SIZE
    query = rotate(q_ref[...], cos_ref[...], sin_ref[...], lane)
    q_out[...] = query.astype(BF16)
    keys = twice(k_out[...].astype(F32), second, lane).astype(BF16)
    value = twice(v_out[...].astype(F32), second, lane)
    for start in range(0, tokens, tile):
        seen = start + tile
        total = jnp.zeros((tile, LANES), F32)
        for half in range(2):
            inside = low if half == 0 else ~low
            part = jnp.where(inside[:tile], query[start:seen], 0.0).astype(BF16)
            scores = dot(part, keys[:seen], 1, 1) * scale + mask[start:seen, :seen]
            peak = jnp.max(scores, axis=1, keepdims=True)
            weights = jnp.exp(scores - peak)
            norm = jnp.sum(weights, axis=1, keepdims=True)
            probability = (weights / norm).astype(BF16)
            shown = jnp.where(inside, value, 0.0).astype(BF16)
            total += dot(probability, shown[:seen], 1, 0)
            log_total = peak + jnp.log(norm)
            here = lane[:tile] == 2 * step + half
            lse_ref[start:seen, :] = jnp.where(here, log_total, lse_ref[start:seen, :])
        o_ref[start:seen, :] = total.astype(BF16)


def attention_forward(qkv, cosine, signed_sine, segments, heads, kv_heads):
    tokens = qkv.shape[0]
    steps = heads // 2
    tile = tile_of(tokens, 256)
    fixed = lambda j: (0, 0)
    block = (tokens, LANES)
    scores = heads * tokens * tokens
    return pl.pallas_call(
        functools.partial(attention_forward_kernel, steps // kv_heads, tile),
        grid=(steps,),
        in_specs=[
            pl.BlockSpec(block, lambda j: (0, j)),
            pl.BlockSpec(block, lambda j: (0, steps)),
            pl.BlockSpec(block, lambda j: (0, steps + 1)),
            pl.BlockSpec(block, fixed),
            pl.BlockSpec(block, fixed),
            pl.BlockSpec((1, tokens), fixed),
            pl.BlockSpec((tokens, 1), fixed),
        ],
        out_specs=[
            pl.BlockSpec(block, lambda j: (0, j)),
            pl.BlockSpec(block, fixed),
            pl.BlockSpec(block, fixed),
            pl.BlockSpec(block, lambda j: (0, j)),
            pl.BlockSpec(block, fixed),
        ],
        out_shape=[
            jax.ShapeDtypeStruct((tokens, heads * HEAD_SIZE), BF16),
            jax.ShapeDtypeStruct(block, BF16),
            jax.ShapeDtypeStruct(block, BF16),
            jax.ShapeDtypeStruct((tokens, heads * HEAD_SIZE), BF16),
            jax.ShapeDtypeStruct(block, F32),
        ],
        scratch_shapes=[pltpu.VMEM((tokens, tokens), F32)],
        compiler_params=params(),
        cost_estimate=cost(4 * scores * HEAD_SIZE, 6 * tokens * qkv.shape[1], scores),
    )(qkv, qkv, qkv, cosine, signed_sine, segments[None, :], segments[:, None])


def attention_backward_kernel(
    part, steps, tile, q_ref, k_ref, v_ref, o_ref, do_ref, lse_ref, cos_ref, sin_ref,
    seg_row, seg_col, *refs,
):
    if part:
        key_before, value_before, out_ref, mask, key_part, value_part = refs
    else:
        out_ref, key_out, value_out, mask, key_part, value_part = refs
    step = pl.program_id(0)
    tokens = q_ref.shape[0]
    lane = lax.broadcasted_iota(jnp.int32, (tokens, LANES), 1)
    low = lane < HEAD_SIZE
    scale = HEAD_SIZE**-0.5

    @pl.when(step == 0)
    def _():
        row = lax.broadcasted_iota(jnp.int32, (tokens, tokens), 0)
        col = lax.broadcasted_iota(jnp.int32, (tokens, tokens), 1)
        allowed = (seg_col[...] == seg_row[...]) & (col <= row)
        mask[...] = jnp.where(allowed, 0.0, MASKED)
        key_part[...] = jnp.zeros_like(key_part)
        value_part[...] = jnp.zeros_like(value_part)

    @pl.when(step < steps)
    def _():
        keys = twice(k_ref[...].astype(F32), part == 1, lane)
        value = twice(v_ref[...].astype(F32), part == 1, lane).astype(BF16)
        keys_low = keys.astype(BF16)
        given = do_ref[...].astype(F32)
        product = given * o_ref[...].astype(F32)
        query = q_ref[...].astype(F32)
        for start in range(0, tokens, tile):
            seen = start + tile
            total = jnp.zeros((tile, LANES), F32)
            for half in range(2):
                inside = low if half == 0 else ~low
                near = inside[:tile]
                part_q = jnp.where(near, query[start:seen], 0.0).astype(BF16)
                grad = jnp.where(near, given[start:seen], 0.0).astype(BF16)
                terms = jnp.sum(
                    jnp.where(near, product[start:seen], 0.0), axis=1, keepdims=True
                )
                here = lane[:tile] == 2 * (step + part * steps) + half
                log_total = jnp.sum(
                    jnp.where(here, lse_ref[start:seen, :], 0.0), axis=1, keepdims=True
                )
                scores = dot(part_q, keys_low[:seen], 1, 1) * scale + mask[start:seen, :seen]
                weights = jnp.exp(scores - log_total)
                slope = dot(grad, value[:seen], 1, 1)
                back = (weights * (slope - terms)).astype(BF16)
                shown = jnp.where(inside, keys, 0.0).astype(BF16)
                total += dot(back, shown[:seen], 1, 0)
                key_part[:seen, :] += dot(back, part_q, 0, 0)
                value_part[:seen, :] += dot(weights.astype(BF16), grad, 0, 0)
            out_ref[start:seen, :] = rotate(
                total * scale, cos_ref[start:seen, :], -sin_ref[start:seen, :], lane[:tile]
            ).astype(BF16)

    def folded(sums):
        return sums[...] + pltpu.roll(sums[...], HEAD_SIZE, 1)

    if part == 0:

        @pl.when(step == steps - 1)
        def _():
            key_out[...] = folded(key_part)
            value_out[...] = folded(value_part)

    else:

        @pl.when(step == steps)
        def _():
            total = jnp.where(low, key_before[...], folded(key_part))
            out_ref[...] = rotate(
                total * scale, cos_ref[...], -sin_ref[...], lane
            ).astype(BF16)

        @pl.when(step == steps + 1)
        def _():
            out_ref[...] = jnp.where(low, value_before[...], folded(value_part)).astype(BF16)


def attention_backward(
    part, before, query, keys, value, attended, attended_grad, log_total, cosine, signed_sine,
    segments,
):
    tokens, width = query.shape
    steps = width // LANES // 2
    tile = tile_of(tokens, 256)
    fixed_block = lambda j: (0, 0)
    moving = lambda j: (0, part * steps + jnp.minimum(j, steps - 1))
    block = (tokens, LANES)
    scores = width // HEAD_SIZE * tokens * tokens // 2
    outs = pl.BlockSpec(block, lambda j: (0, j))
    shapes = jax.ShapeDtypeStruct((tokens, (steps + 2 * part) * LANES), BF16)
    if part == 0:
        outs = [outs] + [pl.BlockSpec(block, fixed_block)] * 2
        shapes = [shapes] + [jax.ShapeDtypeStruct(block, F32)] * 2
    return pl.pallas_call(
        functools.partial(attention_backward_kernel, part, steps, tile),
        grid=(steps + 2 * part,),
        in_specs=[
            pl.BlockSpec(block, moving),
            pl.BlockSpec(block, fixed_block),
            pl.BlockSpec(block, fixed_block),
            pl.BlockSpec(block, moving),
            pl.BlockSpec(block, moving),
            pl.BlockSpec(block, fixed_block),
            pl.BlockSpec(block, fixed_block),
            pl.BlockSpec(block, fixed_block),
            pl.BlockSpec((1, tokens), fixed_block),
            pl.BlockSpec((tokens, 1), fixed_block),
        ]
        + [pl.BlockSpec(block, fixed_block)] * len(before),
        out_specs=outs,
        out_shape=shapes,
        scratch_shapes=[pltpu.VMEM((tokens, tokens), F32)] + [pltpu.VMEM(block, F32)] * 2,
        compiler_params=params(),
        cost_estimate=cost(10 * scores * HEAD_SIZE, 4 * tokens * width, scores),
    )(
        query, keys, value, attended, attended_grad, log_total, cosine, signed_sine,
        segments[None, :], segments[:, None], *before,
    )


def gathered_order(ring, width):
    rows = ring.width // ring.dp
    block = ring.pairs * ring.cores
    places = []
    for begin in range(0, width // rows, block):
        for p in range(ring.pairs):
            for c in range(ring.cores):
                places.append((begin + p * ring.cores + c, begin + c * ring.pairs + p))
    return [(slice(a * rows, (a + 1) * rows), slice(b * rows, (b + 1) * rows)) for a, b in places]


def hidden_kernel(ring, pieces, *refs):
    gate_ref, up_ref, down_ref, out, hidden, given = refs[pieces:]

    @pl.when(pl.program_id(0) == 0)
    def _():
        for held, parts in ((hidden, refs[: pieces - 2]), (given, refs[pieces - 2 : pieces])):
            at = 0
            for part in parts:
                for place, found in gathered_order(ring, part.shape[1]):
                    held[at : at + part.shape[0], found] = part[:, place]
                at += part.shape[0]

    for begin in range(0, out.shape[2], 256):
        here = slice(begin, min(begin + 256, out.shape[2]))
        gate = dot(hidden[...], gate_ref[:, here], 1, 0)
        up = dot(hidden[...], up_ref[:, here], 1, 0)
        grad = dot(given[...], down_ref[:, here], 1, 0)
        sigma = jax.nn.sigmoid(gate)
        swish = gate * sigma
        out[0, :, here] = (swish * up).astype(BF16)
        out[1, :, here] = (grad * up * sigma * (1.0 + gate * (1.0 - sigma))).astype(BF16)
        out[2, :, here] = (grad * swish).astype(BF16)


def hidden_units(ring, hidden_two, grad_low, weights):
    tokens, width = sum(part.shape[0] for part in grad_low), weights.shape[0]
    units = weights.shape[-1] // 3
    tile = 256 if units % 256 == 0 else units
    count = units // tile
    pieces = [*hidden_two, *grad_low]

    def columns(part):
        buffers = pl.Buffered(1 if count == 1 else 2)
        return pl.BlockSpec(
            (width, tile), lambda j: (0, part * count + j), pipeline_mode=buffers
        )

    return pl.pallas_call(
        functools.partial(hidden_kernel, ring, len(pieces)),
        grid=(count,),
        in_specs=[
            pl.BlockSpec(part.shape, lambda j: (0, 0), pipeline_mode=pl.Buffered(1))
            for part in pieces
        ]
        + [columns(0), columns(1), columns(2)],
        out_specs=pl.BlockSpec((3, tokens, tile), lambda j: (0, 0, j)),
        out_shape=jax.ShapeDtypeStruct((3, tokens, units), BF16),
        scratch_shapes=[pltpu.VMEM((tokens, width), BF16)] * 2,
        compiler_params=params(),
        cost_estimate=cost(6 * tokens * width * units, 6 * width * units, tokens * units),
    )(*pieces, weights, weights, weights)


def back_kernel(ring, parts, has_start, *refs):
    values, weights = refs[:parts], refs[parts : 2 * parts]
    total = dot(values[0][...], weights[0][...], 1, 1)
    for value, weight in zip(values[1:], weights[1:]):
        total += dot(value[...], weight[...], 1, 1)
    tokens = refs[-1].shape[0]
    for at, out in ((0, refs[-2]), (1, refs[-1])):
        for place, found in gathered_order(ring, out.shape[1]):
            part = total[at * tokens : (at + 1) * tokens, found]
            if has_start:
                part += refs[2 * parts + at][:, place].astype(F32)
            out[:, place] = part.astype(out.dtype)


def back_project(ring, terms, start=None, piece=0, pieces=1):
    both = terms[0][0].shape[1]
    tokens = both // 2
    width = terms[0][2].shape[0]
    tile = min(512, width // pieces)
    count = width // pieces // tile

    def chosen(pick, units):
        return pl.BlockSpec((None, both, units), lambda j: (pick, 0, 0))

    def columns(part, units):
        return pl.BlockSpec((tile, units), lambda j: (piece * count + j, part))

    sizes = [values.shape[2] for values, _, _, _ in terms]
    begin = pl.BlockSpec((tokens, tile), lambda j: (0, piece * count + j))
    return pl.pallas_call(
        functools.partial(back_kernel, ring, len(terms), start is not None),
        grid=(count,),
        in_specs=[chosen(pick, units) for (_, pick, _, _), units in zip(terms, sizes)]
        + [columns(part, units) for (_, _, _, part), units in zip(terms, sizes)]
        + ([begin] * 2 if start is not None else []),
        out_specs=[pl.BlockSpec((tokens, tile), lambda j: (0, j))] * 2,
        out_shape=[jax.ShapeDtypeStruct((tokens, count * tile), BF16)] * 2,
        compiler_params=params(),
        cost_estimate=cost(
            2 * both * width * sum(sizes) // pieces, 2 * width * sum(sizes) // pieces
        ),
    )(
        *(values for values, _, _, _ in terms),
        *(weights for _, _, weights, _ in terms),
        *(start if start is not None else ()),
    )


def deal(turned, rows, core, mine, give):
    for block in range(turned.shape[0] // (2 * rows)):
        begin = 2 * block * rows
        first, second = turned[begin : begin + rows], turned[begin + rows : begin + 2 * rows]
        here = slice(block * rows, (block + 1) * rows)
        mine[here, :] = jnp.where(core[0] == 0, first, second)
        give[here, :] = jnp.where(core[0] == 0, second, first)


def transpose_kernel(rows, core, *refs):
    turned = jnp.concatenate([ref[...] for ref in refs[:-2]], 0).T
    deal(turned, rows, core, *refs[-2:])


def transposed(values, rows, core):
    tokens, width = values[0].shape
    tile = tile_of(width, 512)
    count = len(values)
    return pl.pallas_call(
        functools.partial(transpose_kernel, rows),
        grid_spec=pltpu.PrefetchScalarGridSpec(
            num_scalar_prefetch=1,
            grid=(width // tile,),
            in_specs=[pl.BlockSpec((tokens, tile), lambda j, c: (0, j))] * count,
            out_specs=[pl.BlockSpec((tile // 2, count * tokens), lambda j, c: (j, 0))] * 2,
        ),
        out_shape=[jax.ShapeDtypeStruct((width // 2, count * tokens), BF16)] * 2,
        compiler_params=params(),
        cost_estimate=cost(0, 4 * tokens * width * count),
    )(core, *values)


def grad_kernel(layout, lefts, rights, has_extra, pieces, where, *refs):
    own_left, got_left = refs[:lefts], refs[lefts : 2 * lefts]
    own_right = refs[2 * lefts : 2 * lefts + rights]
    got_right = refs[2 * lefts + rights : 2 * lefts + 2 * rights]
    step = pl.program_id(0)
    rows, tokens = own_left[0].shape[-2:]
    height = own_left[0].shape[0] * own_left[0].shape[1] * rows
    for left, right, begin, end in layout:

        @pl.when((step >= begin) & (step < end))
        def _():
            shape = (height, tokens)
            total = dot(own_left[left][...].reshape(shape), own_right[right][...], 1, 0)
            total += dot(got_left[left][...].reshape(shape), got_right[right][...], 1, 0)
            if has_extra:
                total += refs[2 * lefts + 2 * rights][...].astype(F32)
            if pieces == 0:
                refs[-1][...] = total.astype(BF16)
                return
            outs, held = refs[-pieces - 1 : -1], refs[-1]
            held[...] = total
            for shift, out in enumerate(outs):
                start = pl.multiple_of(where[1 + shift] * rows, rows)
                out[...] = held[pl.ds(start, rows), :].astype(BF16)


def weight_grad(where, own_left, got_left, rights, extra=None, split=False, whole=False):
    groups, pairs, rows, tokens = own_left[0].shape
    taken = pairs if whole else 1
    height = groups * taken * rows
    tile = math.gcd(*(own.shape[-1] for _, own, _, _ in rights))
    tile //= next(n for n in range(1, tile) if tile // n <= (1024 if whole else 1536) and tile % (n * LANES) == 0)
    layout, columns, begin = [], [], 0
    for k, (side, own, _, pick) in enumerate(rights):
        count = own.shape[-1] // tile
        layout.append((side, k, begin, begin + count))
        columns.append(
            pl.BlockSpec(
                (None, tokens, tile),
                functools.partial(
                    lambda j, w, p, b, n: (p, 0, jnp.clip(j - b, 0, n - 1)),
                    p=pick,
                    b=begin,
                    n=count,
                ),
            )
        )
        begin += count
    left = pl.BlockSpec(
        (groups, taken, rows, tokens), lambda j, w: (0, 0 if whole else w[0], 0, 0)
    )
    out = pl.BlockSpec((height, tile), lambda j, w: (0, j))
    args = [*own_left, *got_left, *(r[1] for r in rights), *(r[2] for r in rights)]
    specs = [left] * (2 * len(own_left)) + columns * 2
    shapes = jax.ShapeDtypeStruct((height, begin * tile), BF16)
    outs, scratch, pieces = out, [], 0
    if extra is not None:
        args.append(extra)
        specs.append(out)
    if split:
        pieces = groups
        outs = [pl.BlockSpec((rows, tile), lambda j, w: (0, j))] * groups
        shapes = [jax.ShapeDtypeStruct((rows, begin * tile), BF16)] * groups
        scratch = [pltpu.VMEM((height, tile), F32)]
    return pl.pallas_call(
        functools.partial(
            grad_kernel, tuple(layout), len(own_left), len(rights), extra is not None, pieces
        ),
        grid_spec=pltpu.PrefetchScalarGridSpec(
            num_scalar_prefetch=1,
            grid=(begin,),
            in_specs=specs,
            out_specs=outs,
            scratch_shapes=scratch,
        ),
        out_shape=shapes,
        compiler_params=params(),
        cost_estimate=cost(
            4 * height * tokens * begin * tile, 2 * (height + 2 * tokens) * begin * tile
        ),
    )(where, *args)


def middle_kernel(parts, held_rows, core, *refs):
    middle, given, gain = refs[2 * parts : 2 * parts + 3]
    grad_out, low_out, mine, give, sums_out = refs[2 * parts + 3 :]
    total = jnp.concatenate(
        [refs[k][...].astype(F32) + refs[parts + k][...].astype(F32) for k in range(parts)], 1
    )
    normed, inverse = normalize(middle[...])

    @pl.when(pl.program_id(0) == 0)
    def _():
        sums_out[...] = jnp.zeros_like(sums_out)

    sums_out[...] += jnp.sum(total * normed, axis=0, keepdims=True)
    scaled = total * gain[...]
    grad = given[...] + inverse * (
        scaled - normed * jnp.mean(scaled * normed, axis=-1, keepdims=True)
    )
    grad_out[...] = grad
    low_out[...] = grad.astype(BF16)
    deal(grad.astype(BF16).T, held_rows, core, mine, give)


def middle_backward(own, other, middle, out_grad, gain, held_rows, core):
    tokens, width = middle.shape
    tile = 128
    rows = pl.BlockSpec((tile, width), lambda i, c: (i, 0))
    line = pl.BlockSpec((1, width), lambda i, c: (0, 0))
    turned = pl.BlockSpec((width // 2, tile), lambda i, c: (0, i))
    pieces = [pl.BlockSpec((tile, part.shape[1]), lambda i, c: (i, 0)) for part in own]
    return pl.pallas_call(
        functools.partial(middle_kernel, len(own), held_rows),
        grid_spec=pltpu.PrefetchScalarGridSpec(
            num_scalar_prefetch=1,
            grid=(tokens // tile,),
            in_specs=pieces * 2 + [rows, rows, line],
            out_specs=[rows, rows, turned, turned, line],
        ),
        out_shape=[
            jax.ShapeDtypeStruct((tokens, width), F32),
            jax.ShapeDtypeStruct((tokens, width), BF16),
            jax.ShapeDtypeStruct((width // 2, tokens), BF16),
            jax.ShapeDtypeStruct((width // 2, tokens), BF16),
            jax.ShapeDtypeStruct((1, width), F32),
        ],
        compiler_params=params(),
        cost_estimate=cost(20 * tokens * width, 20 * tokens * width),
    )(core, *own, *other, middle, out_grad, gain[None])


def input_kernel(own, other, block_input, grad, gain, out):
    total = own[...].astype(F32) + other[...].astype(F32)
    normed, inverse = normalize(block_input[...].astype(F32))
    scaled = total * gain[...]
    out[...] = grad[...] + inverse * (
        scaled - normed * jnp.mean(scaled * normed, axis=-1, keepdims=True)
    )


def input_backward(own, other, block_input, middle_grad, gain):
    tokens, width = middle_grad.shape
    rows = pl.BlockSpec((128, width), lambda i: (i, 0))
    return pl.pallas_call(
        input_kernel,
        grid=(tokens // 128,),
        in_specs=[rows] * 4 + [pl.BlockSpec((1, width), lambda i: (0, 0))],
        out_specs=rows,
        out_shape=jax.ShapeDtypeStruct((tokens, width), F32),
        compiler_params=params(),
        cost_estimate=cost(10 * tokens * width, 14 * tokens * width),
    )(own, other, block_input, middle_grad, gain[None])


def joined_kernel(sizes, half, pair, *refs):
    mine, sent, (gate, up, down) = refs[: len(sizes)], refs[len(sizes) : -3], refs[-3:]
    for index in range(2):
        begin = index * half
        for own, other, size in zip(mine, sent, sizes):
            part = jnp.where(pair[0] == index, own[...].astype(F32), other[...].astype(F32))
            down[begin : begin + size, :] = part[:, :size].T
            gate[:, begin : begin + size] = part[:, size : 2 * size]
            up[:, begin : begin + size] = part[:, 2 * size :]
            begin += size


def joined(pair, mine, sent):
    rows = sent[0].shape[0]
    sizes = [part.shape[1] // 3 for part in sent]
    half = sum(sizes)
    wide = jax.ShapeDtypeStruct((rows, 2 * half), F32)
    return pl.pallas_call(
        functools.partial(joined_kernel, sizes, half),
        grid_spec=pltpu.PrefetchScalarGridSpec(
            num_scalar_prefetch=1,
            grid=(1,),
            in_specs=[
                pl.BlockSpec((None, *part.shape[1:]), lambda i, p: (p[0], 0, 0)) for part in mine
            ]
            + [pl.BlockSpec(part.shape, lambda i, p: (0, 0)) for part in sent],
            out_specs=[
                pl.BlockSpec((rows, 2 * half), lambda i, p: (0, 0)),
                pl.BlockSpec((rows, 2 * half), lambda i, p: (0, 0)),
                pl.BlockSpec((2 * half, rows), lambda i, p: (0, 0)),
            ],
        ),
        out_shape=[wide, wide, jax.ShapeDtypeStruct((2 * half, rows), F32)],
        compiler_params=params(),
        cost_estimate=cost(0, 40 * rows * half),
    )(pair, *mine, *sent)


def per_device(
    ring,
    block_input,
    segment_ids,
    position_ids,
    attn_gain,
    w_query,
    key_projection_weight,
    value_projection_weight,
    w_out,
    mlp_gain,
    w_gate,
    w_up,
    w_down,
    out_grad,
):
    seq_len, width = block_input.shape
    ring.width = width
    rows = w_query.shape[0]
    q_cols, kv_cols = w_query.shape[1], key_projection_weight.shape[1]
    heads, kv_heads = q_cols // HEAD_SIZE, kv_cols // HEAD_SIZE
    hidden = w_gate.shape[1]
    me = lax.axis_index("dp")
    core = me % ring.cores
    pair = (me // ring.cores) % ring.pairs
    my_group = me // (ring.cores * ring.pairs)

    def swap_tensor(low):
        return lax.ppermute(low, "tensor", [(0, 1), (1, 0)])

    def tensor_sum(low, after=None):
        other = swap_tensor(low)
        if after is not None:
            other = fixed((other, after))[0]
        return low.astype(F32) + other.astype(F32)

    gains = jnp.pad(jnp.stack([attn_gain, mlp_gain], 1), ((0, 0), (0, LANES - 2)))
    qkv_cols = q_cols + 2 * kv_cols
    first = lax.all_gather(
        jnp.concatenate(
            [w_query, key_projection_weight, value_projection_weight, w_out.T, gains], 1
        ),
        "dp",
        axis=0,
        tiled=True,
    )
    half = hidden // ring.pairs
    cut = (half // LANES * 6 // 11) * LANES
    bounds = ((0, cut), (cut, half))
    local = jnp.stack([w_gate, w_up, w_down.T], 1).reshape(rows, 3, ring.pairs, half)

    def of_pair(index):
        return lax.dynamic_index_in_dim(local, index, 2, keepdims=False)

    kept = of_pair(pair)
    sent = ring.swap_pair(of_pair(1 - pair))
    both = jnp.stack([jnp.where(pair == 0, kept, sent), jnp.where(pair == 0, sent, kept)], 0)
    weights_a, weights_b = [
        lax.all_gather(
            both[..., a:b].reshape(ring.pairs * rows, 3 * (b - a)),
            "dp",
            axis=0,
            tiled=True,
            axis_index_groups=ring.column_list(),
        )
        for a, b in bounds
    ]
    full_qkv = first[:, :qkv_cols]
    out_t = first[:, qkv_cols : qkv_cols + w_out.shape[0]]
    gain_rows = first[:, qkv_cols + w_out.shape[0] :].T.astype(F32)
    gain_one, gain_two = gain_rows[0], gain_rows[1]

    def left_side(*values):
        return left_rows(*transposed(values, rows, core[None]))

    def left_rows(mine, give):
        shape = (ring.groups, ring.pairs, rows, -1)
        return mine.reshape(shape), ring.swap_core(give.reshape(shape))

    targets = [(my_group + shift) % ring.groups for shift in range(ring.groups)]
    far = jnp.stack([1 - pair, *targets]).astype(jnp.int32)
    near = jnp.stack([pair, *targets]).astype(jnp.int32)

    residual_in = block_input.astype(F32)
    normed_one, _ = normalize(residual_in)
    hidden_one = fixed((normed_one * gain_one).astype(BF16))
    half_dim = HEAD_SIZE // 2
    frequency = 10000.0 ** (-(jnp.arange(half_dim, dtype=F32) * 2.0 / HEAD_SIZE))
    angles = position_ids.astype(F32)[:, None] * frequency[None, :]
    cosine, sine = jnp.cos(angles), jnp.sin(angles)
    cosine = jnp.concatenate([cosine] * 4, 1)
    signed_sine = jnp.concatenate([-sine, sine, -sine, sine], 1)
    qkv = dot(hidden_one, full_qkv, 1, 0)

    def both_pairs(values):
        return values, ring.swap_pair(values)

    grad_low = both_pairs(fixed((out_grad.astype(BF16), qkv))[0])
    grad_left = left_side(*grad_low)
    query, keys, value, attended, log_total = attention_forward(
        qkv, cosine, signed_sine, segment_ids, heads, kv_heads
    )
    attended_got = ring.swap_core(attended)
    one_left = left_side(hidden_one)
    middles, hiddens = [], []
    for k in range(2):
        part = slice(k * seq_len // 2, (k + 1) * seq_len // 2)
        low = dot(attended[part], out_t, 1, 1, BF16)
        middles.append(residual_in[part] + tensor_sum(low, hiddens[-1][0] if k else None))
        hidden_part = fixed((normalize(middles[k])[0] * gain_two).astype(BF16))
        hiddens.append(both_pairs(hidden_part))
    hidden_two = (hiddens[0][0], hiddens[1][0], hiddens[0][1], hiddens[1][1])
    middle = fixed(jnp.concatenate(middles, 0))
    two_left = left_side(*hidden_two)

    def terms_of(weights):
        terms = hidden_units(ring, hidden_two, grad_low, weights)
        return terms, ring.swap_core(terms)

    def group_sum(part):
        return lax.psum_scatter(
            part, "dp", scatter_dimension=0, tiled=True, axis_index_groups=ring.group_list()
        )

    def gradient(left, rights, direct):
        sides = ([x[0] for x in left], [x[1] for x in left], rights)
        part = weight_grad(far, *sides)
        sent = ring.swap_pair(part)
        parts = weight_grad(near, *sides, sent, split=direct)
        if not direct:
            return part, [group_sum(parts)]
        return part, [parts[0]] + [
            ring.shift_group(parts[shift], shift) for shift in range(1, ring.groups)
        ]

    def summed(parts, begin=0, end=None):
        total = parts[0][:, begin:end].astype(F32)
        for part in parts[1:]:
            total = total + part[:, begin:end].astype(F32)
        return total

    def hidden_grads(terms, got):
        lefts = (grad_left, two_left)
        rights = [(0, terms, got, 0), (1, terms, got, 1), (1, terms, got, 2)]
        part = weight_grad(near, [x[0] for x in lefts], [x[1] for x in lefts], rights, whole=True)
        part = group_sum(part)
        return part.reshape(ring.pairs, rows, -1)

    def for_pair(part):
        other = lax.dynamic_index_in_dim(part, 1 - pair, 0, keepdims=False)
        return ring.swap_pair(other)

    def pair_sum(low, after=None):
        sent = ring.swap_pair(low[1])
        if after is not None:
            sent = fixed((sent, after))[0]
        return (low[0].astype(F32) + sent.astype(F32)).astype(BF16)

    terms_a, got_a = terms_of(weights_a)
    two_part = back_project(ring, [(terms_a, 1, weights_a, 0), (terms_a, 2, weights_a, 1)])
    grads_a = hidden_grads(terms_a, got_a)
    terms_b, got_b = terms_of(weights_b)
    two_own, two_other, low = [], [], None
    for piece in range(PIECES):
        before = low
        low = back_project(
            ring,
            [(terms_b, 1, weights_b, 0), (terms_b, 2, weights_b, 1)],
            two_part,
            piece,
            PIECES,
        )
        low = fixed(pair_sum(low, before))
        two_own.append(low)
        two_other.append(swap_tensor(low))
    grads_b = hidden_grads(terms_b, got_b)
    mlp_low = back_project(ring, [(terms_a, 0, weights_a, 2), (terms_b, 0, weights_b, 2)])
    mlp_low = pair_sum(mlp_low)

    middle_grad, middle_low, mine, give, mlp_gain_part = middle_backward(
        two_own, two_other, middle, out_grad, gain_two, rows, core[None]
    )
    attended_grad = dot(middle_low, out_t, 1, 0, BF16)
    middle_left = left_rows(mine, give)
    qkv_back, qkv_got, before = [], [], ()
    for part in range(2):
        back, *before = jax.tree.leaves(
            attention_backward(
                part, before, query, keys, value, attended, attended_grad, log_total,
                cosine, signed_sine, segment_ids,
            )
        )
        qkv_back.append(back)
        qkv_got.append(ring.swap_core(back))
    block_output = middle + tensor_sum(mlp_low, qkv_back[1])
    rights = [(0, attended[None], attended_got[None], 0)]
    _, out_parts = gradient([middle_left], rights, False)
    qkv_parts = []
    far_rows = []
    for part, (back, got) in enumerate(zip(qkv_back, qkv_got)):
        rights = [(0, back[None], got[None], 0)]
        far_part, parts = gradient([one_left], rights, True)
        far_rows.append(far_part)
        qkv_parts.append(parts)
    qkv_back = jnp.concatenate(qkv_back, 1)
    one_low = dot(fixed((qkv_back, far_rows[0]))[0], full_qkv, 1, 1, BF16)
    attn_gain_part = jnp.sum(one_low.astype(F32) * normed_one, axis=0)
    one_other = swap_tensor(one_low)
    one_other = fixed((one_other, attn_gain_part, block_output))[0]
    input_grad = input_backward(one_low, one_other, block_input, middle_grad, gain_one)

    other = fixed((swap_tensor(attn_gain_part), qkv_parts[1][0]))[0]
    attn_gain_part = attn_gain_part + other
    small = jnp.stack([attn_gain_part, mlp_gain_part[0]], 0)
    small = small + ring.swap_core(small)
    small = small + ring.swap_pair(small)
    small = small.reshape(2, ring.groups, ring.pairs, ring.cores, rows)
    small = lax.dynamic_index_in_dim(small, core, 3, keepdims=False)
    small = lax.dynamic_index_in_dim(small, pair, 2, keepdims=False)
    own = lax.dynamic_index_in_dim(small, my_group, 1, keepdims=False)
    for shift in range(1, ring.groups):
        target = (my_group + shift) % ring.groups
        piece = lax.dynamic_index_in_dim(small, target, 1, keepdims=False)
        own = own + ring.shift_group(piece, shift)

    qkv_parts, out_parts, _ = fixed((qkv_parts, out_parts, own))
    sent = [for_pair(grads_a), for_pair(grads_b)]
    gate_grad, up_grad, down_grad = joined(pair[None], [grads_a, grads_b], sent)

    return (
        block_output,
        input_grad,
        own[0],
        jnp.concatenate([summed(qkv_parts[0]), summed(qkv_parts[1], 0, q_cols // 2)], 1),
        summed(qkv_parts[1], q_cols // 2, q_cols // 2 + kv_cols),
        summed(qkv_parts[1], q_cols // 2 + kv_cols),
        summed(out_parts).T,
        own[1],
        gate_grad,
        up_grad,
        down_grad,
    )


PIECES = 4


def solution(mesh):
    ring = Ring(mesh.shape["dp"], mesh.shape["tensor"])
    rows, line, down, across = P("dp", None), P("dp"), P("dp", "tensor"), P("tensor", "dp")
    ins = (rows, line, line, line, down, down, down, across, line, down, down, across, rows)
    outs = (rows, rows, line, down, down, down, across, line, down, down, across)

    def body(*args):
        return per_device(ring, *args)

    return jax.shard_map(
        body,
        mesh=mesh,
        in_specs=ins,
        out_specs=outs,
        check_vma=False,
    )
```

```python
import functools
import math

import jax
import jax.numpy as jnp
from jax import lax
from jax.experimental import pallas as pl
from jax.experimental.pallas import tpu as pltpu
from jax.sharding import PartitionSpec as P


fixed = lax.optimization_barrier

HEAD_SIZE = 64
EPSILON = 1e-05
MASKED = -1e30
LANES = 128
F32 = jnp.float32
BF16 = jnp.bfloat16


def dot(a, b, ca, cb, out=F32):
    return lax.dot_general(a, b, (((ca,), (cb,)), ((), ())), preferred_element_type=out)


def cost(flops, moved, exps=0):
    return pl.CostEstimate(flops=int(flops), bytes_accessed=int(moved), transcendentals=int(exps))


def params(count=1):
    return pltpu.CompilerParams(
        dimension_semantics=("arbitrary",) * count, vmem_limit_bytes=60 * 1024 * 1024
    )


def normalize(values):
    inverse = lax.rsqrt(jnp.mean(values * values, axis=-1, keepdims=True) + EPSILON)
    return (values * inverse, inverse)


def tile_of(width, most):
    tile = most
    while width % tile:
        tile //= 2
    return tile


class Ring:
    def __init__(self, dp, tensor):
        self.dp, self.tensor, self.width = dp, tensor, None
        self.cores = self.pairs = 2
        self.groups = dp // 4

    def at(self, g, p, c):
        return (g * self.pairs + p) * self.cores + c

    def members(self):
        return [
            (g, p, c)
            for g in range(self.groups)
            for p in range(self.pairs)
            for c in range(self.cores)
        ]

    def move(self, value, where):
        return lax.ppermute(
            value, "dp", [(self.at(*m), self.at(*where(*m))) for m in self.members()]
        )

    def swap_core(self, value):
        return self.move(value, lambda g, p, c: (g, p, 1 - c))

    def swap_pair(self, value):
        return self.move(value, lambda g, p, c: (g, 1 - p, c))

    def shift_group(self, value, shift):
        return self.move(value, lambda g, p, c: ((g + shift) % self.groups, p, c))

    def column_list(self):
        return [
            [self.at(g, p, c) for g in range(self.groups) for c in range(self.cores)]
            for p in range(self.pairs)
        ]

    def group_list(self):
        return [
            [self.at(g, p, c) for g in range(self.groups)]
            for p in range(self.pairs)
            for c in range(self.cores)
        ]


def rotate(values, cosine, signed_sine, lane):
    ahead = pltpu.roll(values, LANES - HEAD_SIZE // 2, 1)
    behind = pltpu.roll(values, HEAD_SIZE // 2, 1)
    crossed = jnp.where(lane % HEAD_SIZE < HEAD_SIZE // 2, ahead, behind)
    return values * cosine + crossed * signed_sine


def twice(values, second, lane):
    other = pltpu.roll(values, HEAD_SIZE, 1)
    low = lane < HEAD_SIZE
    return jnp.where(second, jnp.where(low, other, values), jnp.where(low, values, other))


def attention_forward_kernel(
    per_kv, tile, q_ref, k_ref, v_ref, cos_ref, sin_ref, seg_row, seg_col,
    q_out, k_out, v_out, o_ref, lse_ref, mask,
):
    step = pl.program_id(0)
    tokens = q_ref.shape[0]
    lane = lax.broadcasted_iota(jnp.int32, (tokens, LANES), 1)
    scale = HEAD_SIZE**-0.5

    @pl.when(step == 0)
    def _():
        row = lax.broadcasted_iota(jnp.int32, (tokens, tokens), 0)
        col = lax.broadcasted_iota(jnp.int32, (tokens, tokens), 1)
        allowed = (seg_col[...] == seg_row[...]) & (col <= row)
        mask[...] = jnp.where(allowed, 0.0, MASKED)
        k_out[...] = rotate(k_ref[...], cos_ref[...], sin_ref[...], lane).astype(BF16)
        v_out[...] = v_ref[...].astype(BF16)
        lse_ref[...] = jnp.zeros_like(lse_ref)

    second = step // per_kv == 1
    low = lane < HEAD_SIZE
    query = rotate(q_ref[...], cos_ref[...], sin_ref[...], lane)
    q_out[...] = query.astype(BF16)
    keys = twice(k_out[...].astype(F32), second, lane).astype(BF16)
    value = twice(v_out[...].astype(F32), second, lane)
    for start in range(0, tokens, tile):
        seen = start + tile
        total = jnp.zeros((tile, LANES), F32)
        for half in range(2):
            inside = low if half == 0 else ~low
            part = jnp.where(inside[:tile], query[start:seen], 0.0).astype(BF16)
            scores = dot(part, keys[:seen], 1, 1) * scale + mask[start:seen, :seen]
            peak = jnp.max(scores, axis=1, keepdims=True)
            weights = jnp.exp(scores - peak)
            norm = jnp.sum(weights, axis=1, keepdims=True)
            probability = (weights / norm).astype(BF16)
            shown = jnp.where(inside, value, 0.0).astype(BF16)
            total += dot(probability, shown[:seen], 1, 0)
            log_total = peak + jnp.log(norm)
            here = lane[:tile] == 2 * step + half
            lse_ref[start:seen, :] = jnp.where(here, log_total, lse_ref[start:seen, :])
        o_ref[start:seen, :] = total.astype(BF16)


def attention_forward(qkv, cosine, signed_sine, segments, heads, kv_heads):
    tokens = qkv.shape[0]
    steps = heads // 2
    tile = tile_of(tokens, 256)
    fixed = lambda j: (0, 0)
    block = (tokens, LANES)
    scores = heads * tokens * tokens
    return pl.pallas_call(
        functools.partial(attention_forward_kernel, steps // kv_heads, tile),
        grid=(steps,),
        in_specs=[
            pl.BlockSpec(block, lambda j: (0, j)),
            pl.BlockSpec(block, lambda j: (0, steps)),
            pl.BlockSpec(block, lambda j: (0, steps + 1)),
            pl.BlockSpec(block, fixed),
            pl.BlockSpec(block, fixed),
            pl.BlockSpec((1, tokens), fixed),
            pl.BlockSpec((tokens, 1), fixed),
        ],
        out_specs=[
            pl.BlockSpec(block, lambda j: (0, j)),
            pl.BlockSpec(block, fixed),
            pl.BlockSpec(block, fixed),
            pl.BlockSpec(block, lambda j: (0, j)),
            pl.BlockSpec(block, fixed),
        ],
        out_shape=[
            jax.ShapeDtypeStruct((tokens, heads * HEAD_SIZE), BF16),
            jax.ShapeDtypeStruct(block, BF16),
            jax.ShapeDtypeStruct(block, BF16),
            jax.ShapeDtypeStruct((tokens, heads * HEAD_SIZE), BF16),
            jax.ShapeDtypeStruct(block, F32),
        ],
        scratch_shapes=[pltpu.VMEM((tokens, tokens), F32)],
        compiler_params=params(),
        cost_estimate=cost(4 * scores * HEAD_SIZE, 6 * tokens * qkv.shape[1], scores),
    )(qkv, qkv, qkv, cosine, signed_sine, segments[None, :], segments[:, None])


def attention_backward_kernel(
    part, steps, tile, q_ref, k_ref, v_ref, o_ref, do_ref, lse_ref, cos_ref, sin_ref,
    seg_row, seg_col, *refs,
):
    if part:
        key_before, value_before, out_ref, mask, key_part, value_part = refs
    else:
        out_ref, key_out, value_out, mask, key_part, value_part = refs
    step = pl.program_id(0)
    tokens = q_ref.shape[0]
    lane = lax.broadcasted_iota(jnp.int32, (tokens, LANES), 1)
    low = lane < HEAD_SIZE
    scale = HEAD_SIZE**-0.5

    @pl.when(step == 0)
    def _():
        row = lax.broadcasted_iota(jnp.int32, (tokens, tokens), 0)
        col = lax.broadcasted_iota(jnp.int32, (tokens, tokens), 1)
        allowed = (seg_col[...] == seg_row[...]) & (col <= row)
        mask[...] = jnp.where(allowed, 0.0, MASKED)
        key_part[...] = jnp.zeros_like(key_part)
        value_part[...] = jnp.zeros_like(value_part)

    @pl.when(step < steps)
    def _():
        keys = twice(k_ref[...].astype(F32), part == 1, lane)
        value = twice(v_ref[...].astype(F32), part == 1, lane).astype(BF16)
        keys_low = keys.astype(BF16)
        given = do_ref[...].astype(F32)
        product = given * o_ref[...].astype(F32)
        query = q_ref[...].astype(F32)
        for start in range(0, tokens, tile):
            seen = start + tile
            total = jnp.zeros((tile, LANES), F32)
            for half in range(2):
                inside = low if half == 0 else ~low
                near = inside[:tile]
                part_q = jnp.where(near, query[start:seen], 0.0).astype(BF16)
                grad = jnp.where(near, given[start:seen], 0.0).astype(BF16)
                terms = jnp.sum(
                    jnp.where(near, product[start:seen], 0.0), axis=1, keepdims=True
                )
                here = lane[:tile] == 2 * (step + part * steps) + half
                log_total = jnp.sum(
                    jnp.where(here, lse_ref[start:seen, :], 0.0), axis=1, keepdims=True
                )
                scores = dot(part_q, keys_low[:seen], 1, 1) * scale + mask[start:seen, :seen]
                weights = jnp.exp(scores - log_total)
                slope = dot(grad, value[:seen], 1, 1)
                back = (weights * (slope - terms)).astype(BF16)
                shown = jnp.where(inside, keys, 0.0).astype(BF16)
                total += dot(back, shown[:seen], 1, 0)
                key_part[:seen, :] += dot(back, part_q, 0, 0)
                value_part[:seen, :] += dot(weights.astype(BF16), grad, 0, 0)
            out_ref[start:seen, :] = rotate(
                total * scale, cos_ref[start:seen, :], -sin_ref[start:seen, :], lane[:tile]
            ).astype(BF16)

    def folded(sums):
        return sums[...] + pltpu.roll(sums[...], HEAD_SIZE, 1)

    if part == 0:

        @pl.when(step == steps - 1)
        def _():
            key_out[...] = folded(key_part)
            value_out[...] = folded(value_part)

    else:

        @pl.when(step == steps)
        def _():
            total = jnp.where(low, key_before[...], folded(key_part))
            out_ref[...] = rotate(
                total * scale, cos_ref[...], -sin_ref[...], lane
            ).astype(BF16)

        @pl.when(step == steps + 1)
        def _():
            out_ref[...] = jnp.where(low, value_before[...], folded(value_part)).astype(BF16)


def attention_backward(
    part, before, query, keys, value, attended, attended_grad, log_total, cosine, signed_sine,
    segments,
):
    tokens, width = query.shape
    steps = width // LANES // 2
    tile = tile_of(tokens, 256)
    fixed_block = lambda j: (0, 0)
    moving = lambda j: (0, part * steps + jnp.minimum(j, steps - 1))
    block = (tokens, LANES)
    scores = width // HEAD_SIZE * tokens * tokens // 2
    outs = pl.BlockSpec(block, lambda j: (0, j))
    shapes = jax.ShapeDtypeStruct((tokens, (steps + 2 * part) * LANES), BF16)
    if part == 0:
        outs = [outs] + [pl.BlockSpec(block, fixed_block)] * 2
        shapes = [shapes] + [jax.ShapeDtypeStruct(block, F32)] * 2
    return pl.pallas_call(
        functools.partial(attention_backward_kernel, part, steps, tile),
        grid=(steps + 2 * part,),
        in_specs=[
            pl.BlockSpec(block, moving),
            pl.BlockSpec(block, fixed_block),
            pl.BlockSpec(block, fixed_block),
            pl.BlockSpec(block, moving),
            pl.BlockSpec(block, moving),
            pl.BlockSpec(block, fixed_block),
            pl.BlockSpec(block, fixed_block),
            pl.BlockSpec(block, fixed_block),
            pl.BlockSpec((1, tokens), fixed_block),
            pl.BlockSpec((tokens, 1), fixed_block),
        ]
        + [pl.BlockSpec(block, fixed_block)] * len(before),
        out_specs=outs,
        out_shape=shapes,
        scratch_shapes=[pltpu.VMEM((tokens, tokens), F32)] + [pltpu.VMEM(block, F32)] * 2,
        compiler_params=params(),
        cost_estimate=cost(10 * scores * HEAD_SIZE, 4 * tokens * width, scores),
    )(
        query, keys, value, attended, attended_grad, log_total, cosine, signed_sine,
        segments[None, :], segments[:, None], *before,
    )


def gathered_order(ring, width):
    rows = ring.width // ring.dp
    block = ring.pairs * ring.cores
    places = []
    for begin in range(0, width // rows, block):
        for p in range(ring.pairs):
            for c in range(ring.cores):
                places.append((begin + p * ring.cores + c, begin + c * ring.pairs + p))
    return [(slice(a * rows, (a + 1) * rows), slice(b * rows, (b + 1) * rows)) for a, b in places]


def hidden_kernel(ring, pieces, *refs):
    gate_ref, up_ref, down_ref, out, hidden, given = refs[pieces:]

    @pl.when(pl.program_id(0) == 0)
    def _():
        for held, parts in ((hidden, refs[: pieces - 2]), (given, refs[pieces - 2 : pieces])):
            at = 0
            for part in parts:
                for place, found in gathered_order(ring, part.shape[1]):
                    held[at : at + part.shape[0], found] = part[:, place]
                at += part.shape[0]

    for begin in range(0, out.shape[2], 256):
        here = slice(begin, min(begin + 256, out.shape[2]))
        gate = dot(hidden[...], gate_ref[:, here], 1, 0)
        up = dot(hidden[...], up_ref[:, here], 1, 0)
        grad = dot(given[...], down_ref[:, here], 1, 0)
        sigma = jax.nn.sigmoid(gate)
        swish = gate * sigma
        out[0, :, here] = (swish * up).astype(BF16)
        out[1, :, here] = (grad * up * sigma * (1.0 + gate * (1.0 - sigma))).astype(BF16)
        out[2, :, here] = (grad * swish).astype(BF16)


def hidden_units(ring, hidden_two, grad_low, weights):
    tokens, width = sum(part.shape[0] for part in grad_low), weights.shape[0]
    units = weights.shape[-1] // 3
    tile = 256 if units % 256 == 0 else units
    count = units // tile
    pieces = [*hidden_two, *grad_low]

    def columns(part):
        buffers = pl.Buffered(1 if count == 1 else 2)
        return pl.BlockSpec(
            (width, tile), lambda j: (0, part * count + j), pipeline_mode=buffers
        )

    return pl.pallas_call(
        functools.partial(hidden_kernel, ring, len(pieces)),
        grid=(count,),
        in_specs=[
            pl.BlockSpec(part.shape, lambda j: (0, 0), pipeline_mode=pl.Buffered(1))
            for part in pieces
        ]
        + [columns(0), columns(1), columns(2)],
        out_specs=pl.BlockSpec((3, tokens, tile), lambda j: (0, 0, j)),
        out_shape=jax.ShapeDtypeStruct((3, tokens, units), BF16),
        scratch_shapes=[pltpu.VMEM((tokens, width), BF16)] * 2,
        compiler_params=params(),
        cost_estimate=cost(6 * tokens * width * units, 6 * width * units, tokens * units),
    )(*pieces, weights, weights, weights)


def back_kernel(ring, parts, has_start, *refs):
    values, weights = refs[:parts], refs[parts : 2 * parts]
    total = dot(values[0][...], weights[0][...], 1, 1)
    for value, weight in zip(values[1:], weights[1:]):
        total += dot(value[...], weight[...], 1, 1)
    tokens = refs[-1].shape[0]
    for at, out in ((0, refs[-2]), (1, refs[-1])):
        for place, found in gathered_order(ring, out.shape[1]):
            part = total[at * tokens : (at + 1) * tokens, found]
            if has_start:
                part += refs[2 * parts + at][:, place].astype(F32)
            out[:, place] = part.astype(out.dtype)


def back_project(ring, terms, start=None, piece=0, pieces=1):
    both = terms[0][0].shape[1]
    tokens = both // 2
    width = terms[0][2].shape[0]
    tile = min(512, width // pieces)
    count = width // pieces // tile

    def chosen(pick, units):
        return pl.BlockSpec((None, both, units), lambda j: (pick, 0, 0))

    def columns(part, units):
        return pl.BlockSpec((tile, units), lambda j: (piece * count + j, part))

    sizes = [values.shape[2] for values, _, _, _ in terms]
    begin = pl.BlockSpec((tokens, tile), lambda j: (0, piece * count + j))
    return pl.pallas_call(
        functools.partial(back_kernel, ring, len(terms), start is not None),
        grid=(count,),
        in_specs=[chosen(pick, units) for (_, pick, _, _), units in zip(terms, sizes)]
        + [columns(part, units) for (_, _, _, part), units in zip(terms, sizes)]
        + ([begin] * 2 if start is not None else []),
        out_specs=[pl.BlockSpec((tokens, tile), lambda j: (0, j))] * 2,
        out_shape=[jax.ShapeDtypeStruct((tokens, count * tile), BF16)] * 2,
        compiler_params=params(),
        cost_estimate=cost(
            2 * both * width * sum(sizes) // pieces, 2 * width * sum(sizes) // pieces
        ),
    )(
        *(values for values, _, _, _ in terms),
        *(weights for _, _, weights, _ in terms),
        *(start if start is not None else ()),
    )


def transpose_kernel(*refs):
    refs[-1][...] = jnp.concatenate([ref[...] for ref in refs[:-1]], 0).T


def transposed(values):
    tokens, width = values[0].shape
    tile = tile_of(width, 512)
    count = len(values)
    return pl.pallas_call(
        transpose_kernel,
        grid=(width // tile,),
        in_specs=[pl.BlockSpec((tokens, tile), lambda j: (0, j))] * count,
        out_specs=pl.BlockSpec((tile, count * tokens), lambda j: (j, 0)),
        out_shape=jax.ShapeDtypeStruct((width, count * tokens), values[0].dtype),
        compiler_params=params(),
        cost_estimate=cost(0, 4 * tokens * width * count),
    )(*values)


def grad_kernel(layout, lefts, rights, has_extra, pieces, where, *refs):
    own_left, got_left = refs[:lefts], refs[lefts : 2 * lefts]
    own_right = refs[2 * lefts : 2 * lefts + rights]
    got_right = refs[2 * lefts + rights : 2 * lefts + 2 * rights]
    step = pl.program_id(0)
    rows, tokens = own_left[0].shape[-2:]
    height = own_left[0].shape[0] * own_left[0].shape[1] * rows
    for left, right, begin, end in layout:

        @pl.when((step >= begin) & (step < end))
        def _():
            shape = (height, tokens)
            total = dot(own_left[left][...].reshape(shape), own_right[right][...], 1, 0)
            total += dot(got_left[left][...].reshape(shape), got_right[right][...], 1, 0)
            if has_extra:
                total += refs[2 * lefts + 2 * rights][...].astype(F32)
            if pieces == 0:
                refs[-1][...] = total.astype(BF16)
                return
            outs, held = refs[-pieces - 1 : -1], refs[-1]
            held[...] = total
            for shift, out in enumerate(outs):
                start = pl.multiple_of(where[2 + shift] * rows, rows)
                out[...] = held[pl.ds(start, rows), :].astype(BF16)


def weight_grad(where, own_left, got_left, rights, extra=None, split=False, whole=False):
    groups, pairs, _, rows, tokens = own_left[0].shape
    taken = pairs if whole else 1
    height = groups * taken * rows
    tile = math.gcd(*(own.shape[-1] for _, own, _, _ in rights))
    tile //= next(n for n in range(1, tile) if tile // n <= (1024 if whole else 1536) and tile % (n * LANES) == 0)
    layout, columns, begin = [], [], 0
    for k, (left, own, _, pick) in enumerate(rights):
        count = own.shape[-1] // tile
        layout.append((left, k, begin, begin + count))
        columns.append(
            pl.BlockSpec(
                (None, tokens, tile),
                functools.partial(
                    lambda j, w, p, b, n: (p, 0, jnp.clip(j - b, 0, n - 1)),
                    p=pick,
                    b=begin,
                    n=count,
                ),
            )
        )
        begin += count
    own = pl.BlockSpec(
        (groups, taken, 1, rows, tokens), lambda j, w: (0, 0 if whole else w[0], w[1], 0, 0)
    )
    got = pl.BlockSpec(
        (groups, taken, rows, tokens), lambda j, w: (0, 0 if whole else w[0], 0, 0)
    )
    out = pl.BlockSpec((height, tile), lambda j, w: (0, j))
    args = [*own_left, *got_left, *(r[1] for r in rights), *(r[2] for r in rights)]
    specs = [own] * len(own_left) + [got] * len(got_left) + columns * 2
    shapes = jax.ShapeDtypeStruct((height, begin * tile), BF16)
    outs, scratch, pieces = out, [], 0
    if extra is not None:
        args.append(extra)
        specs.append(out)
    if split:
        pieces = groups
        outs = [pl.BlockSpec((rows, tile), lambda j, w: (0, j))] * groups
        shapes = [jax.ShapeDtypeStruct((rows, begin * tile), BF16)] * groups
        scratch = [pltpu.VMEM((height, tile), F32)]
    return pl.pallas_call(
        functools.partial(
            grad_kernel, tuple(layout), len(own_left), len(rights), extra is not None, pieces
        ),
        grid_spec=pltpu.PrefetchScalarGridSpec(
            num_scalar_prefetch=1,
            grid=(begin,),
            in_specs=specs,
            out_specs=outs,
            scratch_shapes=scratch,
        ),
        out_shape=shapes,
        compiler_params=params(),
        cost_estimate=cost(
            4 * height * tokens * begin * tile, 2 * (height + 2 * tokens) * begin * tile
        ),
    )(where, *args)


def middle_kernel(parts, *refs):
    middle, given, gain = refs[2 * parts : 2 * parts + 3]
    grad_out, low_out, turned_out, sums_out = refs[2 * parts + 3 :]
    total = jnp.concatenate(
        [refs[k][...].astype(F32) + refs[parts + k][...].astype(F32) for k in range(parts)], 1
    )
    normed, inverse = normalize(middle[...])

    @pl.when(pl.program_id(0) == 0)
    def _():
        sums_out[...] = jnp.zeros_like(sums_out)

    sums_out[...] += jnp.sum(total * normed, axis=0, keepdims=True)
    scaled = total * gain[...]
    grad = given[...] + inverse * (
        scaled - normed * jnp.mean(scaled * normed, axis=-1, keepdims=True)
    )
    grad_out[...] = grad
    low_out[...] = grad.astype(BF16)
    turned_out[...] = grad.astype(BF16).T


def middle_backward(own, other, middle, out_grad, gain):
    tokens, width = middle.shape
    tile = 128
    rows = pl.BlockSpec((tile, width), lambda i: (i, 0))
    line = pl.BlockSpec((1, width), lambda i: (0, 0))
    pieces = [pl.BlockSpec((tile, part.shape[1]), lambda i: (i, 0)) for part in own]
    return pl.pallas_call(
        functools.partial(middle_kernel, len(own)),
        grid=(tokens // tile,),
        in_specs=pieces * 2 + [rows, rows, line],
        out_specs=[rows, rows, pl.BlockSpec((width, tile), lambda i: (0, i)), line],
        out_shape=[
            jax.ShapeDtypeStruct((tokens, width), F32),
            jax.ShapeDtypeStruct((tokens, width), BF16),
            jax.ShapeDtypeStruct((width, tokens), BF16),
            jax.ShapeDtypeStruct((1, width), F32),
        ],
        compiler_params=params(),
        cost_estimate=cost(20 * tokens * width, 20 * tokens * width),
    )(*own, *other, middle, out_grad, gain[None])


def input_kernel(own, other, block_input, grad, gain, out):
    total = own[...].astype(F32) + other[...].astype(F32)
    normed, inverse = normalize(block_input[...].astype(F32))
    scaled = total * gain[...]
    out[...] = grad[...] + inverse * (
        scaled - normed * jnp.mean(scaled * normed, axis=-1, keepdims=True)
    )


def input_backward(own, other, block_input, middle_grad, gain):
    tokens, width = middle_grad.shape
    rows = pl.BlockSpec((128, width), lambda i: (i, 0))
    return pl.pallas_call(
        input_kernel,
        grid=(tokens // 128,),
        in_specs=[rows] * 4 + [pl.BlockSpec((1, width), lambda i: (0, 0))],
        out_specs=rows,
        out_shape=jax.ShapeDtypeStruct((tokens, width), F32),
        compiler_params=params(),
        cost_estimate=cost(10 * tokens * width, 14 * tokens * width),
    )(own, other, block_input, middle_grad, gain[None])


def joined_kernel(sizes, half, pair, *refs):
    mine, sent, (gate, up, down) = refs[: len(sizes)], refs[len(sizes) : -3], refs[-3:]
    for index in range(2):
        begin = index * half
        for own, other, size in zip(mine, sent, sizes):
            part = jnp.where(pair[0] == index, own[...].astype(F32), other[...].astype(F32))
            down[begin : begin + size, :] = part[:, :size].T
            gate[:, begin : begin + size] = part[:, size : 2 * size]
            up[:, begin : begin + size] = part[:, 2 * size :]
            begin += size


def joined(pair, mine, sent):
    rows = sent[0].shape[0]
    sizes = [part.shape[1] // 3 for part in sent]
    half = sum(sizes)
    wide = jax.ShapeDtypeStruct((rows, 2 * half), F32)
    return pl.pallas_call(
        functools.partial(joined_kernel, sizes, half),
        grid_spec=pltpu.PrefetchScalarGridSpec(
            num_scalar_prefetch=1,
            grid=(1,),
            in_specs=[
                pl.BlockSpec((None, *part.shape[1:]), lambda i, p: (p[0], 0, 0)) for part in mine
            ]
            + [pl.BlockSpec(part.shape, lambda i, p: (0, 0)) for part in sent],
            out_specs=[
                pl.BlockSpec((rows, 2 * half), lambda i, p: (0, 0)),
                pl.BlockSpec((rows, 2 * half), lambda i, p: (0, 0)),
                pl.BlockSpec((2 * half, rows), lambda i, p: (0, 0)),
            ],
        ),
        out_shape=[wide, wide, jax.ShapeDtypeStruct((2 * half, rows), F32)],
        compiler_params=params(),
        cost_estimate=cost(0, 40 * rows * half),
    )(pair, *mine, *sent)


def per_device(
    ring,
    block_input,
    segment_ids,
    position_ids,
    attn_gain,
    w_query,
    key_projection_weight,
    value_projection_weight,
    w_out,
    mlp_gain,
    w_gate,
    w_up,
    w_down,
    out_grad,
):
    seq_len, width = block_input.shape
    ring.width = width
    rows = w_query.shape[0]
    q_cols, kv_cols = w_query.shape[1], key_projection_weight.shape[1]
    heads, kv_heads = q_cols // HEAD_SIZE, kv_cols // HEAD_SIZE
    hidden = w_gate.shape[1]
    me = lax.axis_index("dp")
    core = me % ring.cores
    pair = (me // ring.cores) % ring.pairs
    my_group = me // (ring.cores * ring.pairs)

    def swap_tensor(low):
        return lax.ppermute(low, "tensor", [(0, 1), (1, 0)])

    def tensor_sum(low, after=None):
        other = swap_tensor(low)
        if after is not None:
            other = fixed((other, after))[0]
        return low.astype(F32) + other.astype(F32)

    gains = jnp.pad(jnp.stack([attn_gain, mlp_gain], 1), ((0, 0), (0, LANES - 2)))
    qkv_cols = q_cols + 2 * kv_cols
    first = lax.all_gather(
        jnp.concatenate(
            [w_query, key_projection_weight, value_projection_weight, w_out.T, gains], 1
        ),
        "dp",
        axis=0,
        tiled=True,
    )
    half = hidden // ring.pairs
    cut = (half // LANES * 6 // 11) * LANES
    bounds = ((0, cut), (cut, half))
    local = jnp.stack([w_gate, w_up, w_down.T], 1).reshape(rows, 3, ring.pairs, half)

    def of_pair(index):
        return lax.dynamic_index_in_dim(local, index, 2, keepdims=False)

    kept = of_pair(pair)
    sent = ring.swap_pair(of_pair(1 - pair))
    both = jnp.stack([jnp.where(pair == 0, kept, sent), jnp.where(pair == 0, sent, kept)], 0)
    weights_a, weights_b = [
        lax.all_gather(
            both[..., a:b].reshape(ring.pairs * rows, 3 * (b - a)),
            "dp",
            axis=0,
            tiled=True,
            axis_index_groups=ring.column_list(),
        )
        for a, b in bounds
    ]
    full_qkv = first[:, :qkv_cols]
    out_t = first[:, qkv_cols : qkv_cols + w_out.shape[0]]
    gain_rows = first[:, qkv_cols + w_out.shape[0] :].T.astype(F32)
    gain_one, gain_two = gain_rows[0], gain_rows[1]

    def left_side(*values):
        return left_rows(transposed(values))

    def left_rows(turned):
        own = turned.reshape(ring.groups, ring.pairs, ring.cores, rows, -1)
        give = lax.dynamic_index_in_dim(own, 1 - core, 2, keepdims=False)
        return own, ring.swap_core(give)

    targets = [(my_group + shift) % ring.groups for shift in range(ring.groups)]
    far = jnp.stack([1 - pair, core, *targets]).astype(jnp.int32)
    near = jnp.stack([pair, core, *targets]).astype(jnp.int32)

    residual_in = block_input.astype(F32)
    normed_one, _ = normalize(residual_in)
    hidden_one = fixed((normed_one * gain_one).astype(BF16))
    half_dim = HEAD_SIZE // 2
    frequency = 10000.0 ** (-(jnp.arange(half_dim, dtype=F32) * 2.0 / HEAD_SIZE))
    angles = position_ids.astype(F32)[:, None] * frequency[None, :]
    cosine, sine = jnp.cos(angles), jnp.sin(angles)
    cosine = jnp.concatenate([cosine] * 4, 1)
    signed_sine = jnp.concatenate([-sine, sine, -sine, sine], 1)
    qkv = dot(hidden_one, full_qkv, 1, 0)

    def both_pairs(values):
        return values, ring.swap_pair(values)

    grad_low = both_pairs(fixed((out_grad.astype(BF16), qkv))[0])
    grad_left = left_side(*grad_low)
    query, keys, value, attended, log_total = attention_forward(
        qkv, cosine, signed_sine, segment_ids, heads, kv_heads
    )
    attended_got = ring.swap_core(attended)
    one_left = left_side(hidden_one)
    middles, hiddens = [], []
    for k in range(2):
        part = slice(k * seq_len // 2, (k + 1) * seq_len // 2)
        low = dot(attended[part], out_t, 1, 1, BF16)
        middles.append(residual_in[part] + tensor_sum(low, hiddens[-1][0] if k else None))
        hidden_part = fixed((normalize(middles[k])[0] * gain_two).astype(BF16))
        hiddens.append(both_pairs(hidden_part))
    hidden_two = (hiddens[0][0], hiddens[1][0], hiddens[0][1], hiddens[1][1])
    middle = fixed(jnp.concatenate(middles, 0))
    two_left = left_side(*hidden_two)

    def terms_of(weights):
        terms = hidden_units(ring, hidden_two, grad_low, weights)
        return terms, ring.swap_core(terms)

    def group_sum(part):
        return lax.psum_scatter(
            part, "dp", scatter_dimension=0, tiled=True, axis_index_groups=ring.group_list()
        )

    def gradient(left, rights, direct):
        sides = ([x[0] for x in left], [x[1] for x in left], rights)
        part = weight_grad(far, *sides)
        sent = ring.swap_pair(part)
        parts = weight_grad(near, *sides, sent, split=direct)
        if not direct:
            return part, [group_sum(parts)]
        return part, [parts[0]] + [
            ring.shift_group(parts[shift], shift) for shift in range(1, ring.groups)
        ]

    def summed(parts, begin=0, end=None):
        total = parts[0][:, begin:end].astype(F32)
        for part in parts[1:]:
            total = total + part[:, begin:end].astype(F32)
        return total

    def hidden_grads(terms, got):
        lefts = (grad_left, two_left)
        rights = [(0, terms, got, 0), (1, terms, got, 1), (1, terms, got, 2)]
        part = weight_grad(near, [x[0] for x in lefts], [x[1] for x in lefts], rights, whole=True)
        part = group_sum(part)
        return part.reshape(ring.pairs, rows, -1)

    def for_pair(part):
        other = lax.dynamic_index_in_dim(part, 1 - pair, 0, keepdims=False)
        return ring.swap_pair(other)

    def pair_sum(low, after=None):
        sent = ring.swap_pair(low[1])
        if after is not None:
            sent = fixed((sent, after))[0]
        return (low[0].astype(F32) + sent.astype(F32)).astype(BF16)

    terms_a, got_a = terms_of(weights_a)
    two_part = back_project(ring, [(terms_a, 1, weights_a, 0), (terms_a, 2, weights_a, 1)])
    grads_a = hidden_grads(terms_a, got_a)
    terms_b, got_b = terms_of(weights_b)
    two_own, two_other, low = [], [], None
    for piece in range(PIECES):
        before = low
        low = back_project(
            ring,
            [(terms_b, 1, weights_b, 0), (terms_b, 2, weights_b, 1)],
            two_part,
            piece,
            PIECES,
        )
        low = fixed(pair_sum(low, before))
        two_own.append(low)
        two_other.append(swap_tensor(low))
    grads_b = hidden_grads(terms_b, got_b)
    mlp_low = back_project(ring, [(terms_a, 0, weights_a, 2), (terms_b, 0, weights_b, 2)])
    mlp_low = pair_sum(mlp_low)

    middle_grad, middle_low, middle_turned, mlp_gain_part = middle_backward(
        two_own, two_other, middle, out_grad, gain_two
    )
    attended_grad = dot(middle_low, out_t, 1, 0, BF16)
    middle_left = left_rows(middle_turned)
    qkv_back, qkv_got, before = [], [], ()
    for part in range(2):
        back, *before = jax.tree.leaves(
            attention_backward(
                part, before, query, keys, value, attended, attended_grad, log_total,
                cosine, signed_sine, segment_ids,
            )
        )
        qkv_back.append(back)
        qkv_got.append(ring.swap_core(back))
    block_output = middle + tensor_sum(mlp_low, qkv_back[1])
    rights = [(0, attended[None], attended_got[None], 0)]
    _, out_parts = gradient([middle_left], rights, False)
    qkv_parts = []
    far_rows = []
    for part, (back, got) in enumerate(zip(qkv_back, qkv_got)):
        rights = [(0, back[None], got[None], 0)]
        far_part, parts = gradient([one_left], rights, True)
        far_rows.append(far_part)
        qkv_parts.append(parts)
    qkv_back = jnp.concatenate(qkv_back, 1)
    one_low = dot(fixed((qkv_back, far_rows[0]))[0], full_qkv, 1, 1, BF16)
    attn_gain_part = jnp.sum(one_low.astype(F32) * normed_one, axis=0)
    one_other = swap_tensor(one_low)
    one_other = fixed((one_other, attn_gain_part, block_output))[0]
    input_grad = input_backward(one_low, one_other, block_input, middle_grad, gain_one)

    other = fixed((swap_tensor(attn_gain_part), qkv_parts[1][0]))[0]
    attn_gain_part = attn_gain_part + other
    small = jnp.stack([attn_gain_part, mlp_gain_part[0]], 0)
    small = small + ring.swap_core(small)
    small = small + ring.swap_pair(small)
    small = small.reshape(2, ring.groups, ring.pairs, ring.cores, rows)
    small = lax.dynamic_index_in_dim(small, core, 3, keepdims=False)
    small = lax.dynamic_index_in_dim(small, pair, 2, keepdims=False)
    own = lax.dynamic_index_in_dim(small, my_group, 1, keepdims=False)
    for shift in range(1, ring.groups):
        target = (my_group + shift) % ring.groups
        piece = lax.dynamic_index_in_dim(small, target, 1, keepdims=False)
        own = own + ring.shift_group(piece, shift)

    qkv_parts, out_parts, _ = fixed((qkv_parts, out_parts, own))
    sent = [for_pair(grads_a), for_pair(grads_b)]
    gate_grad, up_grad, down_grad = joined(pair[None], [grads_a, grads_b], sent)

    return (
        block_output,
        input_grad,
        own[0],
        jnp.concatenate([summed(qkv_parts[0]), summed(qkv_parts[1], 0, q_cols // 2)], 1),
        summed(qkv_parts[1], q_cols // 2, q_cols // 2 + kv_cols),
        summed(qkv_parts[1], q_cols // 2 + kv_cols),
        summed(out_parts).T,
        own[1],
        gate_grad,
        up_grad,
        down_grad,
    )


PIECES = 4


def solution(mesh):
    ring = Ring(mesh.shape["dp"], mesh.shape["tensor"])
    rows, line, down, across = P("dp", None), P("dp"), P("dp", "tensor"), P("tensor", "dp")
    ins = (rows, line, line, line, down, down, down, across, line, down, down, across, rows)
    outs = (rows, rows, line, down, down, down, across, line, down, down, across)

    def body(*args):
        return per_device(ring, *args)

    return jax.shard_map(
        body,
        mesh=mesh,
        in_specs=ins,
        out_specs=outs,
        check_vma=False,
    )
```
